32 devices in a mesh: energy: 8 (over z, x), slab: 4 (over y, core).
Axes of the slice: x: 2, y: 2, z: 4, core: 2. Of those that a mesh axis runs over, the one named last changes fastest.
Arguments:
- onsite: float32 [4, 256], P('slab'), may hold values from -1 to 1
- hopping: float32 [4, 256, 256], P('slab'), may hold values from -0.12 to 0.12
- coupling: float32 [4, 256], P('slab'), may hold values from 0.4 to 0.8
- boundary_green: float32 [2, 4, 16, 256, 256], P(None, 'slab', 'energy'), may hold values from -0.09 to 0.09
- damping: float32 [4, 16], P('slab', 'energy'), may hold values from 1.5 to 6
- occupation: float32 [4, 16], P('slab', 'energy'), may hold values from 0 to 1
- tile_map: int32 [4, 128, 128], P('slab'), may hold values from 0 to 255
- prev_potential: float32 [4, 128, 128], P('slab'), may hold values from -6 to 6
Outputs:
- lesser_diag: float32 [4, 16, 256], P('slab', 'energy')
- potential: float32 [4, 128, 128], P('slab', 'energy')
The draws below stay inside these ranges and needn't reach their ends.
All inputs are finite; a program needn't handle non-finite values.
Results may differ from the reference program's by a relative error of at most 0.0003.
Values sent between devices are 32-bit elements; how exact they have to be, the bound alone decides.
No kernel may reach another device: no remote copies, remote signals or barrier semaphores. Data moves between devices by JAX's collectives and lax.ppermute only.
A program may use at most 64 MiB of HBM per device.

```python
import math
import jax
import jax.numpy as jnp
from jax import lax

ORB = 256
GY = 128
GZ = 128
SHIFT = 2
NS_ITERS = 3
SWEEPS = 2
NSLAB = 4
NE = 16


def place_ends(drawn, rng, least, top_value):
    shape = drawn.shape
    place = [jax.random.randint(jax.random.fold_in(rng, axis), (), 0, shape[axis]) for axis in range(len(shape))]
    drawn = drawn.at[tuple(place)].set(least)
    longest = shape.index(max(shape))
    place[longest] = (place[longest] + 1) % shape[longest]
    return drawn.at[tuple(place)].set(top_value)


def level_of(key, dims, shards, least, largest):
    gain, own = 1.0, jax.random.fold_in(key, 6)
    for axis_at, parts in shards:
        steps = jnp.exp(jax.random.uniform(jax.random.fold_in(own, axis_at), (parts,), jnp.float32, least / len(shards), largest / len(shards)))
        gain = gain * jnp.repeat(steps, dims[axis_at] // parts).reshape([-1 if axis == axis_at else 1 for axis in range(len(dims))])
    return gain


def bell_draw(stream_key, dims, scale, most, shards=(), kind=jnp.bfloat16):
    result = jax.random.normal(stream_key, dims, jnp.float32) * scale
    if len(shards) > 0:
        result = level_of(stream_key, dims, shards, -0.22, 0.18) * result
    return jnp.clip(result, min=-most, max=most).astype(kind)


def setup_inputs(seed: int = 0) -> dict:
    splits = jax.random.split(jax.random.key(seed), 9)
    return {
        "onsite": jnp.clip(jax.random.uniform(splits[0], (NSLAB, ORB), jnp.float32, -1.0, 1.0) * level_of(splits[0], (NSLAB, ORB), ((0, 4),), -0.4, 0.0), -1.0, 1.0),
        "hopping": bell_draw(splits[1], (NSLAB, ORB, ORB), 0.02, 0.12, ((0, 4),), jnp.float32),
        "coupling": jnp.clip(0.4 + 0.4 * jax.random.uniform(splits[2], (NSLAB, ORB), jnp.float32) ** level_of(splits[2], (NSLAB, ORB), ((0, 4),), -0.2, 0.2), 0.4, 0.8),
        "boundary_green": bell_draw(splits[3], (2, NSLAB, NE, ORB, ORB), 0.015, 0.09, ((1, 4), (2, 8)), jnp.float32),
        "damping": jnp.clip(jnp.exp(math.log(6.0) - 1.3862944 * jax.random.uniform(splits[4], (NSLAB, NE), jnp.float32) ** level_of(splits[4], (NSLAB, NE), ((0, 4), (1, 8)), -0.2, 0.2)), 1.5, 6.0),
        "occupation": jnp.clip(1.0 * jax.random.uniform(splits[5], (NSLAB, NE), jnp.float32) ** level_of(splits[5], (NSLAB, NE), ((0, 4), (1, 8)), -0.2, 0.2), 0.0, 1.0),
        "tile_map": place_ends(jax.random.randint(splits[6], (NSLAB, GY, GZ), 0, ORB), jax.random.fold_in(splits[6], 1), 0, ORB - 1).astype(jnp.int32),
        "prev_potential": bell_draw(splits[7], (NSLAB, GY, GZ), 1.0, 6.0, ((0, 4),), jnp.float32),
    }


HIGHEST = lax.Precision.HIGHEST
PHONON = 0.5
CHARGE = 2.0
ANISO = 0.05
SCREEN = 0.05


def matmul_complex(left, right):
    def real_product(first, second):
        return jnp.einsum("...ij,...jk->...ik", first, second, precision=HIGHEST)
    return jnp.stack([real_product(left[0], right[0]) - real_product(left[1], right[1]),
                      real_product(left[0], right[1]) + real_product(left[1], right[0])])


def adjoint(matrix):
    return jnp.stack([jnp.swapaxes(matrix[0], -1, -2), -jnp.swapaxes(matrix[1], -1, -2)])


def invert(system, inverse_real, inverse_imag):
    unit_matrix = jnp.eye(system.shape[-1], dtype=jnp.float32)
    approx = jnp.stack([inverse_real[..., None] * unit_matrix, inverse_imag[..., None] * unit_matrix])
    for iteration in range(NS_ITERS):
        product = matmul_complex(system, approx)
        correction = jnp.stack([2.0 * unit_matrix - product[0], -product[1]])
        approx = matmul_complex(approx, correction)
    return approx


def spread_density(density, index_map):
    row_count, column_count = index_map.shape
    block_rows = math.gcd(row_count, 8)
    blocks = index_map.reshape(row_count // block_rows, block_rows, column_count)
    orbitals = jnp.arange(density.shape[0], dtype=jnp.int32)

    def one_block(indices):
        onehot = (indices[..., None] == orbitals).astype(jnp.float32)
        return jnp.einsum("bcn,n->bc", onehot, density, precision=HIGHEST)
    return lax.map(one_block, blocks).reshape(row_count, column_count)


def slab_spectrum(hopping_block, onsite_row, left_green, right_green, left_coupling, self_coupling, damping_row, occupation_row, energies):
    weight_left = left_coupling[:, None] * left_coupling[None, :]
    weight_self = self_coupling[:, None] * self_coupling[None, :]
    self_energy = weight_left * left_green + weight_self * right_green
    diag_real = energies[:, None] - onsite_row[None, :]
    diag_imag = damping_row[:, None] * jnp.ones_like(onsite_row)[None, :]
    modulus = diag_real * diag_real + diag_imag * diag_imag
    inverse_real = diag_real / modulus
    inverse_imag = -diag_imag / modulus
    unit_matrix = jnp.eye(onsite_row.shape[0], dtype=jnp.float32)
    system = jnp.stack([diag_real[..., None] * unit_matrix - hopping_block[None] - self_energy[0],
                        diag_imag[..., None] * unit_matrix - self_energy[1]])
    green_first = invert(system, inverse_real, inverse_imag)
    sigma_less = -occupation_row[None, :, None, None] * (self_energy - adjoint(self_energy))
    lesser_first = matmul_complex(matmul_complex(green_first, sigma_less), adjoint(green_first))
    widths = ((0, 0), (SHIFT, SHIFT), (0, 0), (0, 0))
    wide_green = jnp.pad(green_first, widths)
    wide_less = jnp.pad(lesser_first, widths)
    count = energies.shape[0]
    phonon_green = PHONON * (wide_green[:, :count] + wide_green[:, 2 * SHIFT:])
    phonon_less = PHONON * (wide_less[:, :count] + wide_less[:, 2 * SHIFT:])
    green_second = invert(system - phonon_green, inverse_real, inverse_imag)
    mixed_block = matmul_complex(green_second, sigma_less + phonon_less)
    return jnp.sum(mixed_block[1] * green_second[0] - mixed_block[0] * green_second[1], axis=-1)


def line_solve(right_side, main_diagonal):
    def forward(carry, plane):
        pivot_prev, eliminated_prev = carry
        pivot = main_diagonal - 1.0 / pivot_prev
        factor = main_diagonal - pivot
        eliminated = plane + factor * eliminated_prev
        return (pivot, eliminated), (pivot, eliminated)

    start = (jnp.float32(jnp.inf), jnp.zeros_like(right_side[0]))
    unused, (pivots, eliminated) = lax.scan(forward, start, right_side)

    def backward(after, inputs):
        pivot, plane = inputs
        inverse_pivot = 1.0 / pivot
        value = inverse_pivot * after + plane * inverse_pivot
        return value, value

    unused_last, solved = lax.scan(backward, jnp.zeros_like(right_side[0]), (pivots, eliminated), reverse=True)
    return solved


def reference(onsite, hopping, coupling, boundary_green, damping, occupation, tile_map, prev_potential):
    energies = -2.0 + 4.0 * (jnp.arange(NE, dtype=jnp.int32).astype(jnp.float32) + 0.5) / NE
    green_slabs = jnp.moveaxis(boundary_green, 1, 0)
    zero_slab = jnp.zeros_like(green_slabs[:1])
    left_greens = jnp.concatenate([zero_slab, green_slabs[:-1]], axis=0)
    right_greens = jnp.concatenate([green_slabs[1:], zero_slab], axis=0)
    left_couplings = jnp.concatenate([jnp.zeros_like(coupling[:1]), coupling[:-1]], axis=0)

    def one_slab(inputs):
        hopping_block, onsite_row, left_green, right_green, left_coupling, self_coupling, damping_row, occupation_row = inputs
        return slab_spectrum(hopping_block, onsite_row, left_green, right_green, left_coupling, self_coupling, damping_row, occupation_row, energies)

    lesser_diag = lax.map(one_slab, (hopping, onsite, left_greens, right_greens, left_couplings, coupling, damping, occupation))
    density = (4.0 / NE) * jnp.sum(lesser_diag, axis=1)
    source = CHARGE * lax.map(lambda pair: spread_density(pair[0], pair[1]), (density, tile_map))
    main_diagonal = 2.0 + 4.0 * ANISO + SCREEN
    potential = prev_potential
    for sweep_index in range(SWEEPS):
        padded = jnp.pad(potential, ((0, 0), (1, 1), (1, 1)))
        beside = padded[:, 2:, 1:-1] + padded[:, :-2, 1:-1] + padded[:, 1:-1, 2:] + padded[:, 1:-1, :-2]
        potential = line_solve(source + ANISO * beside, main_diagonal)
    return lesser_diag, potential
```

```python
import functools

import jax
import jax.numpy as jnp
from jax import lax
from jax.experimental import pallas as pl
from jax.experimental.pallas import tpu as pltpu
from jax.sharding import PartitionSpec as P

SHIFT = 2
SWEEPS = 2
PHONON = 0.5
CHARGE = 2.0
ANISO = 0.05
SCREEN = 0.05
MAIN_DIAGONAL = 2.0 + 4.0 * ANISO + SCREEN
LANES = 128
SUBLANES = 8
HALO = 4
VMEM_BYTES = 48 * 1024 * 1024

f32 = jnp.float32
bf16 = jnp.bfloat16
DEVICES = ("energy", "slab")


def parts(matrix):
    high = matrix.astype(bf16)
    return high, (matrix - high.astype(f32)).astype(bf16)


def left_of(matrix):
    real, imag = parts(matrix[0]), parts(matrix[1])
    return [jnp.concatenate([r, i], axis=1) for r, i in zip(real, imag)]


def right_of(matrix):
    real, imag = parts(matrix[0]), parts(matrix[1])
    return [
        jnp.concatenate(
            [jnp.concatenate([r, i], axis=1), jnp.concatenate([-i, r], axis=1)], axis=0
        )
        for r, i in zip(real, imag)
    ]


def right_adjoint_of(matrix):
    real, imag = parts(matrix[0]), parts(matrix[1])
    return [
        jnp.concatenate(
            [jnp.concatenate([r, i], axis=1), jnp.concatenate([-i, r], axis=1)], axis=0
        )
        for r, i in zip(real, imag)
    ]


def product(left, right, transposed=False):
    contract = (((1,), (1 if transposed else 0,)), ((), ()))

    def dot(a, b):
        return lax.dot_general(a, b, contract, preferred_element_type=f32)

    out = dot(left[0], right[0]) + dot(left[1], right[0]) + dot(left[0], right[1])
    size = out.shape[1] // 2
    return out[:, :size], out[:, size:]


def add(*matrices):
    return sum(m[0] for m in matrices), sum(m[1] for m in matrices)


def as_column(row):
    size = row.shape[1]
    return jnp.broadcast_to(row, (SUBLANES, size)).T[:, 0:1]


def start_of(energy, onsite, damping):
    real = energy - onsite
    modulus = real * real + damping * damping
    present = damping > 0.0
    modulus = jnp.where(present, modulus, 1.0)
    return jnp.where(present, real / modulus, 0.0), jnp.where(present, -damping / modulus, 0.0)


def scale(matrix, factor):
    return (
        matrix[0] * factor[0] - matrix[1] * factor[1],
        matrix[0] * factor[1] + matrix[1] * factor[0],
    )


def invert(coupled, row, column):
    b1 = scale(coupled, row)
    b1_left = left_of(b1)
    b2 = product(b1_left, right_of(b1))
    b2_right = right_of(b2)
    b4 = product(left_of(b2), b2_right)
    b3 = product(b1_left, b2_right)
    t = add(b1, b2, b3)
    rest = product(left_of(t), right_of(b4))
    size = b1[0].shape[0]
    unit = (
        lax.broadcasted_iota(jnp.int32, (size, size), 0)
        == lax.broadcasted_iota(jnp.int32, (size, size), 1)
    ).astype(f32)
    total = add(t, b4, rest)
    return scale((unit + total[0], total[1]), column)


class Element:
    def __init__(self, message_ref, hopping_ref, onsite_ref, chain, total_energies):
        size = hopping_ref.shape[-1]
        parity = lax.rem(lax.axis_index("energy"), SHIFT)
        index = (SHIFT * chain + parity).astype(f32)
        energy = -2.0 + (4.0 / total_energies) * (index + 0.5)
        self.sigma = (message_ref[0, 0:size, :], message_ref[1, 0:size, :])
        damping = message_ref[0, size : size + 1, :]
        self.occupation = message_ref[0, size + 1 : size + 2, :]
        onsite = onsite_ref[...]
        self.row = start_of(energy, onsite, damping)
        self.column = tuple(as_column(part) for part in self.row)
        self.hopping = hopping_ref[0]

    def lesser_source(self):
        real, imag = self.sigma
        return -self.occupation * (real - real.T), -self.occupation * (imag + imag.T)

    def green(self, phonon=None):
        coupled = (self.hopping + self.sigma[0], self.sigma[1])
        if phonon is not None:
            coupled = add(coupled, phonon)
        return invert(coupled, self.row, self.column)

    def green_and_lesser(self):
        green = self.green()
        mixed = product(left_of(green), right_of(self.lesser_source()))
        lesser = product(left_of(mixed), right_adjoint_of(green), transposed=True)
        return green, lesser

    def lesser_row(self, greens, lessers):
        half = tuple(PHONON * part for part in add(*greens))
        green = self.green(half)
        source = add(self.lesser_source(), tuple(PHONON * part for part in add(*lessers)))
        mixed = product(left_of(green), right_of(source))
        column = jnp.sum(mixed[1] * green[0] - mixed[0] * green[1], axis=1, keepdims=True)
        return jnp.broadcast_to(column, (column.shape[0], LANES)).T[0:1, :]


def chain_places():
    here = lax.axis_index("energy")
    odd = lax.rem(here, 2)
    step = 1 - 2 * odd
    return {"own": here, "pair": here + step, "early": here + 2 * step, "late": here - step}


def vmem():
    return pl.BlockSpec(memory_space=pltpu.VMEM)


def smem():
    return pl.BlockSpec(memory_space=pltpu.SMEM)


def call(kernel, operands, specs, shapes, products=0, **options):
    several = isinstance(shapes, list)
    listed = shapes if several else [shapes]
    size = listed[0].shape[-1] if listed else 0
    bytes_moved = sum(x.size * 4 for x in operands) + sum(x.size * 4 for x in listed)
    return pl.pallas_call(
        kernel,
        out_shape=shapes,
        in_specs=specs,
        out_specs=[vmem() for _ in listed] if several else vmem(),
        compiler_params=pltpu.CompilerParams(vmem_limit_bytes=VMEM_BYTES),
        cost_estimate=pl.CostEstimate(
            flops=products * 24 * size**3, transcendentals=0, bytes_accessed=bytes_moved
        ),
        **options,
    )(*operands)


def split_blocks(boundary_green, coupling, parity):
    planes, _, _, rows, columns = boundary_green.shape

    def kernel(parity_ref, block_ref, coupling_ref, right_ref, left_ref):
        row = coupling_ref[...]
        block = block_ref[0, 0, 0]
        left_ref[0] = block
        right_ref[0] = block * row * as_column(row)

    shape = jax.ShapeDtypeStruct((planes, rows, columns), f32)
    out = pl.BlockSpec((1, rows, columns), lambda i, p: (i, 0, 0))
    return pl.pallas_call(
        kernel,
        out_shape=[shape, shape],
        grid_spec=pltpu.PrefetchScalarGridSpec(
            num_scalar_prefetch=1,
            grid=(planes,),
            in_specs=[
                pl.BlockSpec((1, 1, 1, rows, columns), lambda i, p: (i, 0, p[0], 0, 0)),
                pl.BlockSpec((1, columns), lambda i, p: (0, 0)),
            ],
            out_specs=[out, out],
        ),
    )(parity, boundary_green, coupling)


def self_energy_message(from_left, from_right, coupling, damping, occupation, own):
    planes, rows, columns = from_left.shape

    def kernel(left_ref, right_ref, coupling_ref, damping_ref, occupation_ref, out_ref):
        parity = lax.rem(lax.axis_index("energy"), SHIFT)
        parity = parity if own else 1 - parity
        row = coupling_ref[...]
        weight = row * as_column(row)
        for plane in range(planes):
            out_ref[plane, 0:rows, :] = left_ref[plane] + weight * right_ref[plane]
            which = lax.broadcasted_iota(jnp.int32, (SUBLANES, columns), 0)
            out_ref[plane, rows : rows + SUBLANES, :] = jnp.where(
                which == 0, damping_ref[0, parity], occupation_ref[0, parity]
            )

    return call(
        kernel,
        (from_left, from_right, coupling, damping, occupation),
        [vmem(), vmem(), vmem(), smem(), smem()],
        jax.ShapeDtypeStruct((planes, rows + SUBLANES, columns), f32),
    )


def green_and_lesser(message, hopping, onsite, place, total_energies):
    def kernel(message_ref, hopping_ref, onsite_ref, green_ref, lesser_ref):
        element = Element(
            message_ref, hopping_ref, onsite_ref, chain_places()[place], total_energies
        )
        green, lesser = element.green_and_lesser()
        for plane in range(2):
            green_ref[plane] = green[plane]
            lesser_ref[plane] = lesser[plane]

    size = hopping.shape[-1]
    shape = jax.ShapeDtypeStruct((2, size, size), f32)
    return call(
        kernel, (message, hopping, onsite), [vmem()] * 3, [shape, shape], products=6
    )


def second_pass(outer, inner, green, lesser, hopping, onsite, places, total_energies, other=None):
    size = hopping.shape[-1]
    count = lax.axis_size("energy") * lax.axis_size("slab")

    def kernel(outer_ref, inner_ref, green_ref, lesser_ref, hopping_ref, onsite_ref, *refs):
        chains = chain_places()
        beyond = Element(outer_ref, hopping_ref, onsite_ref, chains[places[0]], total_energies)
        here = Element(inner_ref, hopping_ref, onsite_ref, chains[places[1]], total_energies)
        beyond_green, beyond_lesser = beyond.green_and_lesser()
        row = here.lesser_row(
            [beyond_green, (green_ref[0], green_ref[1])],
            [beyond_lesser, (lesser_ref[0], lesser_ref[1])],
        )
        if other is None:
            refs[0][...] = row
        else:
            other_row = refs[0][...]
            odd = lax.rem(lax.axis_index("energy"), 2) == 1
            first = jnp.where(odd, other_row, row)
            second = jnp.where(odd, row, other_row)
            both = jnp.concatenate([first, second], axis=0)
            refs[1][...] = jnp.broadcast_to(both[None], refs[1].shape)

    operands = [outer, inner, green, lesser, hopping, onsite]
    if other is None:
        shape = jax.ShapeDtypeStruct((1, size), f32)
    else:
        operands.append(other)
        shape = jax.ShapeDtypeStruct((count, 2, size), f32)
    return call(kernel, operands, [vmem()] * len(operands), shape, products=11)


def grid_rows(tile_map, potential):
    rows = tile_map.shape[1] // lax.axis_size("energy")
    first = lax.axis_index("energy") * rows
    both = jnp.stack([tile_map[0].astype(f32), potential[0]])
    both = jnp.pad(both, ((0, 0), (HALO, HALO), (0, 0)))
    return lax.dynamic_slice_in_dim(both, first, rows + 2 * HALO, axis=1)


def relax(diagonals, turns, orbitals, total_energies, grid_total):
    energy_devices, slabs = diagonals.shape[:2]
    rows, columns = turns[0].shape[1:]
    rows_here = rows - 2 * HALO

    def kernel(diagonal_ref, *refs):
        turn_refs = refs[:slabs]
        lesser_ref, potential_ref, grid_ref = refs[slabs:]
        here, slab = lax.axis_index("energy"), lax.axis_index("slab")
        odd = lax.rem(here, 2)
        for parity in range(2):
            pair = diagonal_ref[here - odd + parity, slab]
            lesser_ref[0, parity : parity + 1, :] = jnp.where(odd == 1, pair[1:2], pair[0:1])
        for turn in range(slabs):
            grid_ref[lax.rem(slab - turn + slabs, slabs)] = turn_refs[turn][...]
        grid_row = (
            lax.broadcasted_iota(jnp.int32, (rows, columns), 0) + here * rows_here - HALO
        )
        inside = (grid_row >= 0) & (grid_row < grid_total)
        column = lax.broadcasted_iota(jnp.int32, (rows, columns), 1)
        sources, potentials = [], []
        for at in range(slabs):
            pair = diagonal_ref[0, at]
            for device in range(1, energy_devices):
                pair = pair + diagonal_ref[device, at]
            density = (4.0 / total_energies) * (pair[0:1] + pair[1:2])
            index = grid_ref[at, 0].astype(jnp.int32)
            found = jnp.zeros((rows, columns), f32)
            for low in range(0, orbitals, LANES):
                table = jnp.broadcast_to(density[:, low : low + LANES], (rows, LANES))
                inner = jnp.clip(index - low, 0, LANES - 1)
                value = jnp.take_along_axis(table, inner, axis=1)
                found = jnp.where((index >= low) & (index < low + LANES), value, found)
            sources.append(CHARGE * found)
            potentials.append(grid_ref[at, 1])
        pivots = [MAIN_DIAGONAL]
        for at in range(1, slabs):
            pivots.append(MAIN_DIAGONAL - 1.0 / pivots[-1])
        for sweep in range(SWEEPS):
            eliminated = []
            for at in range(slabs):
                p = potentials[at]
                beside = (
                    pltpu.roll(p, 1, 0)
                    + pltpu.roll(p, rows - 1, 0)
                    + jnp.where(column == 0, 0.0, pltpu.roll(p, 1, 1))
                    + jnp.where(column == columns - 1, 0.0, pltpu.roll(p, columns - 1, 1))
                )
                right = sources[at] + ANISO * beside
                if at:
                    right = right + (1.0 / pivots[at - 1]) * eliminated[-1]
                eliminated.append(right)
            after = None
            for at in reversed(range(slabs)):
                value = eliminated[at] if after is None else eliminated[at] + after
                after = value * (1.0 / pivots[at])
                potentials[at] = jnp.where(inside, after, 0.0)
        for at in range(slabs):
            grid_ref[at, 0] = potentials[at]
        potential_ref[0] = grid_ref[slab, 0, HALO : HALO + rows_here, :]

    return call(
        kernel,
        (diagonals, *turns),
        [vmem()] * (1 + slabs),
        [
            jax.ShapeDtypeStruct((1, 2, orbitals), f32),
            jax.ShapeDtypeStruct((1, rows_here, columns), f32),
        ],
        scratch_shapes=[pltpu.VMEM((slabs, 2, rows, columns), f32)],
    )


def per_device(
    onsite, hopping, coupling, boundary_green, damping, occupation, tile_map, prev_potential
):
    energy_devices, slabs = lax.axis_size("energy"), lax.axis_size("slab")
    orbitals = onsite.shape[1]
    assert boundary_green.shape[2] == SHIFT and energy_devices % 2 == 0
    total_energies = SHIFT * energy_devices
    odd = lax.rem(lax.axis_index("energy"), 2)

    up = [(i, i + 1) for i in range(slabs - 1)]
    down = [(i + 1, i) for i in range(slabs - 1)]
    last = energy_devices - 1
    pair = [(i, i ^ 1) for i in range(energy_devices)]
    near = [(i, i + 1 if i % 2 else i - 1) for i in range(1, last)]
    far = [(i, i + 2) for i in range(1, last, 2) if i + 2 <= last]
    far += [(i, i - 2) for i in range(2, energy_devices, 2)]

    def exchange(parity, own):
        right, left = split_blocks(boundary_green, coupling, parity[None])
        from_left = lax.ppermute(right, "slab", up)
        from_right = lax.ppermute(left, "slab", down)
        return self_energy_message(from_left, from_right, coupling, damping, occupation, own)

    other = exchange(1 - odd, False)
    mine = exchange(odd, True)
    turns = [grid_rows(tile_map, prev_potential)]
    for turn in range(1, slabs):
        ring = [(i, (i + turn) % slabs) for i in range(slabs)]
        turns.append(lax.ppermute(turns[0], "slab", ring))

    paired = lax.ppermute(other, "energy", pair)
    early = lax.ppermute(mine, "energy", far)
    late = lax.ppermute(other, "energy", near)

    common = (hopping, onsite)
    own_green, own_lesser = green_and_lesser(mine, *common, "own", total_energies)
    pair_green, pair_lesser = green_and_lesser(paired, *common, "pair", total_energies)
    pair_row = second_pass(
        early, paired, own_green, own_lesser, *common, ("early", "pair"), total_energies
    )
    rows = second_pass(
        late, mine, pair_green, pair_lesser, *common, ("late", "own"), total_energies, pair_row
    )
    diagonals = lax.all_to_all(rows, DEVICES, 0, 0)
    diagonals = diagonals.reshape(energy_devices, slabs, 2, orbitals)
    lesser, potential = relax(diagonals, turns, orbitals, total_energies, tile_map.shape[1])
    return lesser, potential


def solution(mesh):
    in_specs = (
        P("slab", None),
        P("slab", None, None),
        P("slab", None),
        P(None, "slab", "energy", None, None),
        P("slab", "energy"),
        P("slab", "energy"),
        P("slab", None, None),
        P("slab", None, None),
    )
    out_specs = (P("slab", "energy", None), P("slab", "energy", None))
    return jax.shard_map(
        per_device, mesh=mesh, in_specs=in_specs, out_specs=out_specs, check_vma=False
    )
```

```python
import functools

import jax
import jax.numpy as jnp
from jax import lax
from jax.experimental import pallas as pl
from jax.experimental.pallas import tpu as pltpu
from jax.sharding import PartitionSpec as P

SHIFT = 2
SWEEPS = 2
PHONON = 0.5
CHARGE = 2.0
ANISO = 0.05
SCREEN = 0.05
MAIN_DIAGONAL = 2.0 + 4.0 * ANISO + SCREEN
LANES = 128
SUBLANES = 8
HALO = 4
VMEM_BYTES = 48 * 1024 * 1024

f32 = jnp.float32
bf16 = jnp.bfloat16
DEVICES = ("energy", "slab")


def parts(matrix):
    high = matrix.astype(bf16)
    return high, (matrix - high.astype(f32)).astype(bf16)


def dot(left, right, transposed=False):
    contract = (((1,), (1 if transposed else 0,)), ((), ()))
    out = [
        lax.dot_general(left[i], right[j], contract, preferred_element_type=f32)
        for i, j in ((0, 0), (1, 0), (0, 1))
    ]
    return out[0] + out[1] + out[2]


def factor(matrix):
    return parts(matrix[0]), parts(matrix[1]), parts(matrix[0] + matrix[1])


def adjoint_factor(matrix):
    return parts(matrix[0]), parts(matrix[1]), parts(matrix[0] - matrix[1])


def product(left, right):
    real, imag, both = (dot(a, b) for a, b in zip(left, right))
    return real - imag, both - real - imag


def adjoint_product(left, right):
    real, imag, both = (dot(a, b, transposed=True) for a, b in zip(left, right))
    return real + imag, both - real + imag


def add(*matrices):
    return sum(m[0] for m in matrices), sum(m[1] for m in matrices)


def as_column(row):
    size = row.shape[1]
    return jnp.broadcast_to(row, (SUBLANES, size)).T[:, 0:1]


def start_of(energy, onsite, damping):
    real = energy - onsite
    modulus = real * real + damping * damping
    present = damping > 0.0
    modulus = jnp.where(present, modulus, 1.0)
    return jnp.where(present, real / modulus, 0.0), jnp.where(present, -damping / modulus, 0.0)


def scale(matrix, factor):
    return (
        matrix[0] * factor[0] - matrix[1] * factor[1],
        matrix[0] * factor[1] + matrix[1] * factor[0],
    )


def invert(coupled, row, column):
    b1 = scale(coupled, row)
    b1_factor = factor(b1)
    b2 = product(b1_factor, b1_factor)
    b2_factor = factor(b2)
    b4 = product(b2_factor, b2_factor)
    b3 = product(b1_factor, b2_factor)
    t = add(b1, b2, b3)
    rest = product(factor(t), factor(b4))
    size = b1[0].shape[0]
    unit = (
        lax.broadcasted_iota(jnp.int32, (size, size), 0)
        == lax.broadcasted_iota(jnp.int32, (size, size), 1)
    ).astype(f32)
    total = add(t, b4, rest)
    return scale((unit + total[0], total[1]), column)


class Element:
    def __init__(self, message_ref, hopping_ref, onsite_ref, chain, total_energies):
        size = hopping_ref.shape[-1]
        parity = lax.rem(lax.axis_index("energy"), SHIFT)
        index = (SHIFT * chain + parity).astype(f32)
        energy = -2.0 + (4.0 / total_energies) * (index + 0.5)
        self.sigma = (message_ref[0, 0:size, :], message_ref[1, 0:size, :])
        damping = message_ref[0, size : size + 1, :]
        self.occupation = message_ref[0, size + 1 : size + 2, :]
        onsite = onsite_ref[...]
        self.row = start_of(energy, onsite, damping)
        self.column = tuple(as_column(part) for part in self.row)
        self.hopping = hopping_ref[0]

    def lesser_source(self):
        real, imag = self.sigma
        return -self.occupation * (real - real.T), -self.occupation * (imag + imag.T)

    def green(self, phonon=None):
        coupled = (self.hopping + self.sigma[0], self.sigma[1])
        if phonon is not None:
            coupled = add(coupled, phonon)
        return invert(coupled, self.row, self.column)

    def green_and_lesser(self):
        green = self.green()
        mixed = product(factor(green), factor(self.lesser_source()))
        return green, adjoint_product(factor(mixed), adjoint_factor(green))

    def lesser_row(self, greens, lessers):
        half = tuple(PHONON * part for part in add(*greens))
        green = self.green(half)
        source = add(self.lesser_source(), tuple(PHONON * part for part in add(*lessers)))
        real, imag = parts(green[0]), parts(green[1])
        source_real, source_imag = parts(source[0]), parts(source[1])
        terms = green[0] * dot(real, source_imag) + green[1] * dot(imag, source_imag)
        terms = terms - 2.0 * green[1] * dot(real, source_real)
        column = jnp.sum(terms, axis=1, keepdims=True)
        return jnp.broadcast_to(column, (column.shape[0], LANES)).T[0:1, :]


def chain_places():
    here = lax.axis_index("energy")
    odd = lax.rem(here, 2)
    step = 1 - 2 * odd
    return {"own": here, "pair": here + step, "early": here + 2 * step, "late": here - step}


def vmem():
    return pl.BlockSpec(memory_space=pltpu.VMEM)


def smem():
    return pl.BlockSpec(memory_space=pltpu.SMEM)


def call(kernel, operands, specs, shapes, products=0, **options):
    several = isinstance(shapes, list)
    listed = shapes if several else [shapes]
    size = listed[0].shape[-1] if listed else 0
    bytes_moved = sum(x.size * 4 for x in operands) + sum(x.size * 4 for x in listed)
    return pl.pallas_call(
        kernel,
        out_shape=shapes,
        in_specs=specs,
        out_specs=[vmem() for _ in listed] if several else vmem(),
        compiler_params=pltpu.CompilerParams(vmem_limit_bytes=VMEM_BYTES),
        cost_estimate=pl.CostEstimate(
            flops=0, transcendentals=0, bytes_accessed=0
        ),
        **options,
    )(*operands)


def block_messages(boundary_green, coupling, damping, occupation):
    planes, _, _, rows, columns = boundary_green.shape

    def kernel(block_ref, coupling_ref, *refs):
        level_refs, other_ref, own_ref, held_refs, sems = refs[:2], refs[2], refs[3], refs[4:6], refs[6]
        parity = lax.rem(lax.axis_index("energy"), SHIFT)
        moves = []
        for which, out_ref in ((1 - parity, other_ref), (parity, own_ref)):
            for plane in range(planes):
                moves.append(
                    (block_ref.at[plane, 0, which], out_ref.at[plane, pl.ds(0, rows)])
                )
        moves.append((coupling_ref, own_ref.at[0, pl.ds(rows, 1)]))
        moves += list(zip(level_refs, held_refs))
        copies = [
            pltpu.make_async_copy(source, target, sems.at[at])
            for at, (source, target) in enumerate(moves)
        ]
        for copy in copies:
            copy.start()
        for copy in copies:
            copy.wait()
        levels = [
            jnp.where(parity == 0, held_ref[0:1, 1:2], held_ref[0:1, 0:1]) for held_ref in held_refs
        ]
        which = lax.broadcasted_iota(jnp.int32, (SUBLANES, columns), 0)
        other_ref[0, rows:, :] = jnp.where(which == 0, levels[0], levels[1])

    operands = (boundary_green, coupling, damping, occupation)
    shape = jax.ShapeDtypeStruct((planes, rows + SUBLANES, columns), f32)
    return call(
        kernel,
        [pltpu.with_memory_space_constraint(x, pltpu.HBM) for x in operands],
        [pl.BlockSpec(memory_space=pltpu.HBM)] * 4,
        [shape, shape],
        scratch_shapes=[
            pltpu.VMEM(damping.shape, f32),
            pltpu.VMEM(damping.shape, f32),
            pltpu.SemaphoreType.DMA((2 * planes + 3,)),
        ],
    )


def self_energy(outer, inner, coupling, coupled, damping, occupation, given=None):
    planes, height, columns = outer.shape
    rows = height - SUBLANES

    def kernel(outer_ref, inner_ref, coupling_ref, *refs):
        out_ref = refs[-1]
        even = lax.rem(lax.axis_index("slab"), 2) == 0
        weights = []
        for at, before in enumerate((even, jnp.logical_not(even))):
            row = jnp.where(before, refs[at][0, rows : rows + 1, :], coupling_ref[...])
            weights.append(row * as_column(row))
        refs = refs[2:]
        if given is None:
            parity = lax.rem(lax.axis_index("energy"), SHIFT)
            which = lax.broadcasted_iota(jnp.int32, (SUBLANES, columns), 0)
            extra = jnp.where(which == 0, refs[0][0, parity], refs[1][0, parity])
        else:
            extra = refs[0][0, rows:, :]
        for plane in range(planes):
            out_ref[plane, 0:rows, :] = (
                weights[0] * outer_ref[plane, 0:rows, :] + weights[1] * inner_ref[plane, 0:rows, :]
            )
            out_ref[plane, rows:, :] = extra

    operands = [outer, inner, coupling, *coupled]
    operands += [damping, occupation] if given is None else [given]
    specs = [vmem()] * 5 + ([smem(), smem()] if given is None else [vmem()])
    return call(kernel, operands, specs, jax.ShapeDtypeStruct(outer.shape, f32))


def green_and_lesser(message, hopping, onsite, place, total_energies):
    def kernel(message_ref, hopping_ref, onsite_ref, green_ref, lesser_ref):
        element = Element(
            message_ref, hopping_ref, onsite_ref, chain_places()[place], total_energies
        )
        green, lesser = element.green_and_lesser()
        for plane in range(2):
            green_ref[plane] = green[plane]
            lesser_ref[plane] = lesser[plane]

    size = hopping.shape[-1]
    shape = jax.ShapeDtypeStruct((2, size, size), f32)
    return call(
        kernel, (message, hopping, onsite), [vmem()] * 3, [shape, shape], products=6
    )


def second_pass(outer, inner, green, lesser, hopping, onsite, places, total_energies, other=None):
    size = hopping.shape[-1]
    count = lax.axis_size("energy") * lax.axis_size("slab")

    def kernel(outer_ref, inner_ref, green_ref, lesser_ref, hopping_ref, onsite_ref, *refs):
        chains = chain_places()
        beyond = Element(outer_ref, hopping_ref, onsite_ref, chains[places[0]], total_energies)
        here = Element(inner_ref, hopping_ref, onsite_ref, chains[places[1]], total_energies)
        beyond_green, beyond_lesser = beyond.green_and_lesser()
        row = here.lesser_row(
            [beyond_green, (green_ref[0], green_ref[1])],
            [beyond_lesser, (lesser_ref[0], lesser_ref[1])],
        )
        if other is None:
            refs[0][...] = row
        else:
            other_row = refs[0][...]
            odd = lax.rem(lax.axis_index("energy"), 2) == 1
            first = jnp.where(odd, other_row, row)
            second = jnp.where(odd, row, other_row)
            both = jnp.concatenate([first, second], axis=0)
            refs[1][...] = jnp.broadcast_to(both[None], refs[1].shape)

    operands = [outer, inner, green, lesser, hopping, onsite]
    if other is None:
        shape = jax.ShapeDtypeStruct((1, size), f32)
    else:
        operands.append(other)
        shape = jax.ShapeDtypeStruct((count, 2, size), f32)
    return call(kernel, operands, [vmem()] * len(operands), shape, products=11)


def grid_rows(tile_map, potential):
    rows = tile_map.shape[1] // lax.axis_size("energy")
    first = lax.axis_index("energy") * rows
    both = jnp.stack([tile_map[0].astype(f32), potential[0]])
    both = jnp.pad(both, ((0, 0), (HALO, HALO), (0, 0)))
    return lax.dynamic_slice_in_dim(both, first, rows + 2 * HALO, axis=1)


def relax(diagonals, turns, orbitals, total_energies, grid_total):
    energy_devices, slabs = diagonals.shape[:2]
    rows, columns = turns[0].shape[1:]
    rows_here = rows - 2 * HALO

    def kernel(diagonal_ref, *refs):
        turn_refs = refs[:slabs]
        lesser_ref, potential_ref, grid_ref = refs[slabs:]
        here, slab = lax.axis_index("energy"), lax.axis_index("slab")
        odd = lax.rem(here, 2)
        for parity in range(2):
            pair = diagonal_ref[here - odd + parity, slab]
            lesser_ref[0, parity : parity + 1, :] = jnp.where(odd == 1, pair[1:2], pair[0:1])
        for turn in range(slabs):
            grid_ref[lax.rem(slab - turn + slabs, slabs)] = turn_refs[turn][...]
        grid_row = (
            lax.broadcasted_iota(jnp.int32, (rows, columns), 0) + here * rows_here - HALO
        )
        inside = (grid_row >= 0) & (grid_row < grid_total)
        column = lax.broadcasted_iota(jnp.int32, (rows, columns), 1)
        sources, potentials = [], []
        for at in range(slabs):
            pair = diagonal_ref[0, at]
            for device in range(1, energy_devices):
                pair = pair + diagonal_ref[device, at]
            density = (4.0 / total_energies) * (pair[0:1] + pair[1:2])
            index = grid_ref[at, 0].astype(jnp.int32)
            found = jnp.zeros((rows, columns), f32)
            for low in range(0, orbitals, LANES):
                table = jnp.broadcast_to(density[:, low : low + LANES], (rows, LANES))
                inner = jnp.clip(index - low, 0, LANES - 1)
                value = jnp.take_along_axis(table, inner, axis=1)
                found = jnp.where((index >= low) & (index < low + LANES), value, found)
            sources.append(CHARGE * found)
            potentials.append(grid_ref[at, 1])
        pivots = [MAIN_DIAGONAL]
        for at in range(1, slabs):
            pivots.append(MAIN_DIAGONAL - 1.0 / pivots[-1])
        for sweep in range(SWEEPS):
            eliminated = []
            for at in range(slabs):
                p = potentials[at]
                beside = (
                    pltpu.roll(p, 1, 0)
                    + pltpu.roll(p, rows - 1, 0)
                    + jnp.where(column == 0, 0.0, pltpu.roll(p, 1, 1))
                    + jnp.where(column == columns - 1, 0.0, pltpu.roll(p, columns - 1, 1))
                )
                right = sources[at] + ANISO * beside
                if at:
                    right = right + (1.0 / pivots[at - 1]) * eliminated[-1]
                eliminated.append(right)
            after = None
            for at in reversed(range(slabs)):
                value = eliminated[at] if after is None else eliminated[at] + after
                after = value * (1.0 / pivots[at])
                potentials[at] = jnp.where(inside, after, 0.0)
        for at in range(slabs):
            grid_ref[at, 0] = potentials[at]
        potential_ref[0] = grid_ref[slab, 0, HALO : HALO + rows_here, :]

    return call(
        kernel,
        (diagonals, *turns),
        [vmem()] * (1 + slabs),
        [
            jax.ShapeDtypeStruct((1, 2, orbitals), f32),
            jax.ShapeDtypeStruct((1, rows_here, columns), f32),
        ],
        scratch_shapes=[pltpu.VMEM((slabs, 2, rows, columns), f32)],
    )


def per_device(
    onsite, hopping, coupling, boundary_green, damping, occupation, tile_map, prev_potential
):
    energy_devices, slabs = lax.axis_size("energy"), lax.axis_size("slab")
    orbitals = onsite.shape[1]
    assert boundary_green.shape[2] == SHIFT and energy_devices % 2 == 0
    total_energies = SHIFT * energy_devices

    swaps = [
        [pair for i in range(low, slabs - 1, 2) for pair in ((i, i + 1), (i + 1, i))]
        for low in (1, 0)
    ]
    last = energy_devices - 1
    pair = [(i, i ^ 1) for i in range(energy_devices)]
    far = [(i, i + 2) for i in range(1, last, 2) if i + 2 <= last]
    far += [(i, i - 2) for i in range(2, energy_devices, 2)]
    near = [(to, i) for i, to in far]

    common = (hopping, onsite)
    other, own = block_messages(boundary_green, coupling, damping, occupation)
    crossed = lax.ppermute(other, "energy", pair)
    own_sides = [lax.ppermute(own, "slab", way) for way in swaps]
    mine = self_energy(*own_sides, coupling, own_sides, damping, occupation)
    early = lax.ppermute(mine, "energy", far)
    pair_sides = [lax.ppermute(crossed, "slab", way) for way in swaps]
    paired = self_energy(*pair_sides, coupling, own_sides, damping, occupation, crossed)
    late = lax.ppermute(paired, "energy", near)
    mine_after, _ = lax.optimization_barrier((mine, paired))
    own_green, own_lesser = green_and_lesser(mine_after, *common, "own", total_energies)
    grid = grid_rows(tile_map, prev_potential)
    own_green, grid = lax.optimization_barrier((own_green, grid))
    turns = [grid]
    for turn in range(1, slabs):
        ring = [(i, (i + turn) % slabs) for i in range(slabs)]
        turns.append(lax.ppermute(turns[0], "slab", ring))

    pair_green, pair_lesser = green_and_lesser(paired, *common, "pair", total_energies)
    early, *turns = lax.optimization_barrier((early, *turns))
    pair_row = second_pass(
        early, paired, own_green, own_lesser, *common, ("early", "pair"), total_energies
    )
    rows = second_pass(
        late, mine, pair_green, pair_lesser, *common, ("late", "own"), total_energies, pair_row
    )
    diagonals = lax.all_to_all(rows, DEVICES, 0, 0)
    diagonals = diagonals.reshape(energy_devices, slabs, 2, orbitals)
    lesser, potential = relax(diagonals, turns, orbitals, total_energies, tile_map.shape[1])
    return lesser, potential


def solution(mesh):
    in_specs = (
        P("slab", None),
        P("slab", None, None),
        P("slab", None),
        P(None, "slab", "energy", None, None),
        P("slab", "energy"),
        P("slab", "energy"),
        P("slab", None, None),
        P("slab", None, None),
    )
    out_specs = (P("slab", "energy", None), P("slab", "energy", None))
    return jax.shard_map(
        per_device, mesh=mesh, in_specs=in_specs, out_specs=out_specs, check_vma=False
    )
```

```python
import functools

import jax
import jax.numpy as jnp
from jax import lax
from jax.experimental import pallas as pl
from jax.experimental.pallas import tpu as pltpu
from jax.sharding import PartitionSpec as P

SHIFT = 2
SWEEPS = 2
PHONON = 0.5
CHARGE = 2.0
ANISO = 0.05
SCREEN = 0.05
MAIN_DIAGONAL = 2.0 + 4.0 * ANISO + SCREEN
LANES = 128
SUBLANES = 8
VMEM_BYTES = 48 * 1024 * 1024

f32 = jnp.float32
bf16 = jnp.bfloat16
DEVICES = ("energy", "slab")


def parts(matrix):
    high = matrix.astype(bf16)
    return high, (matrix - high.astype(f32)).astype(bf16)


def dot(left, right, transposed=False):
    contract = (((1,), (1 if transposed else 0,)), ((), ()))
    out = [
        lax.dot_general(left[i], right[j], contract, preferred_element_type=f32)
        for i, j in ((0, 0), (1, 0), (0, 1))
    ]
    return out[0] + out[1] + out[2]


def factor(matrix):
    return parts(matrix[0]), parts(matrix[1]), parts(matrix[0] + matrix[1])


def adjoint_factor(matrix):
    return parts(matrix[0]), parts(matrix[1]), parts(matrix[0] - matrix[1])


def product(left, right):
    real, imag, both = (dot(a, b) for a, b in zip(left, right))
    return real - imag, both - real - imag


def adjoint_product(left, right):
    real, imag, both = (dot(a, b, transposed=True) for a, b in zip(left, right))
    return real + imag, both - real + imag


def add(*matrices):
    return sum(m[0] for m in matrices), sum(m[1] for m in matrices)


def as_column(row):
    size = row.shape[1]
    return jnp.broadcast_to(row, (SUBLANES, size)).T[:, 0:1]


def start_of(energy, onsite, damping):
    real = energy - onsite
    modulus = real * real + damping * damping
    present = damping > 0.0
    modulus = jnp.where(present, modulus, 1.0)
    return jnp.where(present, real / modulus, 0.0), jnp.where(present, -damping / modulus, 0.0)


def scale(matrix, factor):
    return (
        matrix[0] * factor[0] - matrix[1] * factor[1],
        matrix[0] * factor[1] + matrix[1] * factor[0],
    )


def invert(coupled, row, column):
    b1 = scale(coupled, row)
    b1_factor = factor(b1)
    b2 = product(b1_factor, b1_factor)
    b2_factor = factor(b2)
    b4 = product(b2_factor, b2_factor)
    b3 = product(b1_factor, b2_factor)
    t = add(b1, b2, b3)
    rest = product(factor(t), factor(b4))
    size = b1[0].shape[0]
    unit = (
        lax.broadcasted_iota(jnp.int32, (size, size), 0)
        == lax.broadcasted_iota(jnp.int32, (size, size), 1)
    ).astype(f32)
    total = add(t, b4, rest)
    return scale((unit + total[0], total[1]), column)


def halves(message_ref):
    height, columns = message_ref.shape
    return message_ref.at[pl.ds(columns, height - columns)], message_ref.at[pl.ds(0, columns)]


class Element:
    def __init__(self, message_refs, hopping_ref, onsite_ref, chain, total_energies):
        size = hopping_ref.shape[-1]
        parity = lax.rem(lax.axis_index("energy"), SHIFT)
        index = (SHIFT * chain + parity).astype(f32)
        energy = -2.0 + (4.0 / total_energies) * (index + 0.5)
        real_ref, imag_ref = message_refs if len(message_refs) == 2 else halves(message_refs[0])
        self.sigma = (real_ref[0:size, :], imag_ref[...])
        damping = real_ref[size : size + 1, :]
        self.occupation = real_ref[size + 1 : size + 2, :]
        onsite = onsite_ref[...]
        self.row = start_of(energy, onsite, damping)
        self.column = tuple(as_column(part) for part in self.row)
        self.hopping = hopping_ref[0]

    def lesser_source(self):
        real, imag = self.sigma
        return -self.occupation * (real - real.T), -self.occupation * (imag + imag.T)

    def green(self, phonon=None):
        coupled = (self.hopping + self.sigma[0], self.sigma[1])
        if phonon is not None:
            coupled = add(coupled, phonon)
        return invert(coupled, self.row, self.column)

    def green_and_lesser(self):
        green = self.green()
        mixed = product(factor(green), factor(self.lesser_source()))
        return green, adjoint_product(factor(mixed), adjoint_factor(green))

    def lesser_row(self, greens, lessers):
        half = tuple(PHONON * part for part in add(*greens))
        green = self.green(half)
        source = add(self.lesser_source(), tuple(PHONON * part for part in add(*lessers)))
        real, imag = parts(green[0]), parts(green[1])
        source_real, source_imag = parts(source[0]), parts(source[1])
        terms = green[0] * dot(real, source_imag) + green[1] * dot(imag, source_imag)
        terms = terms - 2.0 * green[1] * dot(real, source_real)
        column = jnp.sum(terms, axis=1, keepdims=True)
        return jnp.broadcast_to(column, (column.shape[0], LANES)).T[0:1, :]


def chain_places():
    here = lax.axis_index("energy")
    odd = lax.rem(here, 2)
    step = 1 - 2 * odd
    return {"own": here, "pair": here + step, "early": here + 2 * step, "late": here - step}


def vmem():
    return pl.BlockSpec(memory_space=pltpu.VMEM)


def smem():
    return pl.BlockSpec(memory_space=pltpu.SMEM)


def call(kernel, operands, specs, shapes, **options):
    several = isinstance(shapes, list)
    return pl.pallas_call(
        kernel,
        out_shape=shapes,
        in_specs=specs,
        out_specs=[vmem() for _ in shapes] if several else vmem(),
        compiler_params=pltpu.CompilerParams(vmem_limit_bytes=VMEM_BYTES),
        cost_estimate=pl.CostEstimate(flops=0, transcendentals=0, bytes_accessed=0),
        **options,
    )(*operands)


def block_messages(boundary_green, coupling, damping, occupation):
    _, _, _, rows, columns = boundary_green.shape

    def kernel(block_ref, coupling_ref, *refs):
        level_refs, (real_ref, imag_ref), own_refs = refs[:2], refs[2:4], refs[4:6]
        held_refs, sems = refs[6:8], refs[8]
        parity = lax.rem(lax.axis_index("energy"), SHIFT)
        moves = [
            (block_ref.at[0, 0, 1 - parity], real_ref.at[pl.ds(0, rows)]),
            *zip(level_refs, held_refs),
            (block_ref.at[1, 0, 1 - parity], imag_ref),
            (block_ref.at[0, 0, parity], own_refs[0].at[pl.ds(0, rows)]),
            (coupling_ref, own_refs[0].at[pl.ds(rows, 1)]),
            (block_ref.at[1, 0, parity], own_refs[1]),
        ]
        copies = [
            pltpu.make_async_copy(source, target, sems.at[at])
            for at, (source, target) in enumerate(moves)
        ]
        for copy in copies:
            copy.start()
        for copy in copies:
            copy.wait()
        levels = [
            jnp.where(parity == 0, held_ref[0:1, 1:2], held_ref[0:1, 0:1]) for held_ref in held_refs
        ]
        which = lax.broadcasted_iota(jnp.int32, (SUBLANES, columns), 0)
        real_ref[rows:, :] = jnp.where(which == 0, levels[0], levels[1])

    operands = (boundary_green, coupling, damping, occupation)
    return call(
        kernel,
        [pltpu.with_memory_space_constraint(x, pltpu.HBM) for x in operands],
        [pl.BlockSpec(memory_space=pltpu.HBM)] * 4,
        [
            jax.ShapeDtypeStruct((height, columns), f32)
            for height in (rows + SUBLANES, rows) * 2
        ],
        scratch_shapes=[
            pltpu.VMEM(damping.shape, f32),
            pltpu.VMEM(damping.shape, f32),
            pltpu.SemaphoreType.DMA((7,)),
        ],
    )


def slab_weights(coupling_ref, side_refs):
    even = lax.rem(lax.axis_index("slab"), 2) == 0
    below = coupling_ref.shape[1]
    weights = []
    for side_ref, before in zip(side_refs, (even, jnp.logical_not(even))):
        row = jnp.where(before, side_ref[below : below + 1, :], coupling_ref[...])
        weights.append(row * as_column(row))
    return weights


def own_self_energy(real_sides, imag_sides, coupling, damping, occupation):
    columns = coupling.shape[1]

    def kernel(*refs):
        real_refs, imag_refs = refs[:2], refs[2:4]
        coupling_ref, damping_ref, occupation_ref, out_ref = refs[4:]
        weights = slab_weights(coupling_ref, real_refs)
        rows = pl.ds(0, columns)
        for low, side_refs in ((0, imag_refs), (columns, real_refs)):
            outer, inner = (w * ref[rows, :] for w, ref in zip(weights, side_refs))
            out_ref[pl.ds(low, columns), :] = outer + inner
        parity = lax.rem(lax.axis_index("energy"), SHIFT)
        which = lax.broadcasted_iota(jnp.int32, (SUBLANES, columns), 0)
        out_ref[2 * columns :, :] = jnp.where(
            which == 0, damping_ref[0, parity], occupation_ref[0, parity]
        )

    return call(
        kernel,
        (*real_sides, *imag_sides, coupling, damping, occupation),
        [vmem()] * 5 + [smem()] * 2,
        jax.ShapeDtypeStruct((2 * columns + SUBLANES, columns), f32),
    )


def pair_self_energy(sides, coupling, own_sides, crossed):
    height, columns = crossed.shape

    def kernel(outer_ref, inner_ref, coupling_ref, own_outer_ref, own_inner_ref, crossed_ref, out_ref):
        outer_weight, inner_weight = slab_weights(coupling_ref, (own_outer_ref, own_inner_ref))
        rows = pl.ds(0, columns)
        out_ref[rows, :] = outer_weight * outer_ref[rows, :] + inner_weight * inner_ref[rows, :]
        if height > columns:
            out_ref[columns:, :] = crossed_ref[columns:, :]

    operands = (*sides, coupling, *own_sides, crossed)
    return call(kernel, operands, [vmem()] * 6, jax.ShapeDtypeStruct((height, columns), f32))


def green_and_lesser(message, hopping, onsite, place, total_energies):
    count = len(message)

    def kernel(*refs):
        hopping_ref, onsite_ref, green_ref, lesser_ref = refs[count:]
        element = Element(
            refs[:count], hopping_ref, onsite_ref, chain_places()[place], total_energies
        )
        green, lesser = element.green_and_lesser()
        for plane in range(2):
            green_ref[plane] = green[plane]
            lesser_ref[plane] = lesser[plane]

    size = hopping.shape[-1]
    shape = jax.ShapeDtypeStruct((2, size, size), f32)
    operands = (*message, hopping, onsite)
    return call(kernel, operands, [vmem()] * len(operands), [shape, shape])


def grid_share(rows_here, energy_devices):
    needed = rows_here + 2 * SWEEPS
    return needed, -(-2 * needed // energy_devices)


def pair_pass(early, paired, green, lesser, hopping, onsite, tile_map, potential, total_energies):
    size = hopping.shape[-1]
    energy_devices, slabs = lax.axis_size("energy"), lax.axis_size("slab")
    grid_total, columns = tile_map.shape[1:]
    rows_here = grid_total // energy_devices
    needed, share = grid_share(rows_here, energy_devices)
    padded = grid_total + 2 * SWEEPS

    def kernel(*refs):
        early_refs, paired_refs, refs = refs[:1], refs[1:3], refs[3:]
        green_ref, lesser_ref, hopping_ref, onsite_ref, tile_ref, potential_ref = refs[:6]
        parcel_ref, grid_ref = refs[6:]
        chains = chain_places()
        here = Element(paired_refs, hopping_ref, onsite_ref, chains["pair"], total_energies)
        beyond = Element(early_refs, hopping_ref, onsite_ref, chains["early"], total_energies)
        beyond_green, beyond_lesser = beyond.green_and_lesser()
        row = here.lesser_row(
            [beyond_green, (green_ref[0], green_ref[1])],
            [beyond_lesser, (lesser_ref[0], lesser_ref[1])],
        )
        border = jnp.zeros((SWEEPS, columns), f32)
        for at, plane in enumerate((potential_ref[0], tile_ref[0].astype(f32))):
            low = at * padded
            grid_ref[low : low + SWEEPS, :] = border
            grid_ref[low + SWEEPS : low + SWEEPS + grid_total, :] = plane
            grid_ref[low + SWEEPS + grid_total : low + padded, :] = border
        first = lax.axis_index("energy") * share
        for to in range(energy_devices):
            pieces = [row]
            for i in range(share):
                place = jnp.minimum(first + i, 2 * needed - 1)
                which = (place >= needed).astype(jnp.int32)
                source = which * (padded - needed) + place + to * rows_here
                pieces.append(grid_ref[pl.ds(source, 1), :])
            parcel = jnp.concatenate(pieces, axis=1)
            for slab in range(slabs):
                parcel_ref[to * slabs + slab, :, size:] = parcel

    operands = [early, *paired, green, lesser, hopping, onsite, tile_map, potential]
    parcels = (energy_devices * slabs, 1, 2 * size + share * columns)
    return call(
        kernel,
        operands,
        [vmem()] * len(operands),
        jax.ShapeDtypeStruct(parcels, f32),
        scratch_shapes=[pltpu.VMEM((2 * padded, columns), f32)],
    )


def own_pass(late, mine, green, lesser, hopping, onsite, parcels, total_energies):
    size = hopping.shape[-1]

    def kernel(*refs):
        late_refs, mine_refs, refs = refs[:2], refs[2:3], refs[3:]
        green_ref, lesser_ref, hopping_ref, onsite_ref, _, parcel_ref = refs
        chains = chain_places()
        here = Element(mine_refs, hopping_ref, onsite_ref, chains["own"], total_energies)
        beyond = Element(late_refs, hopping_ref, onsite_ref, chains["late"], total_energies)
        beyond_green, beyond_lesser = beyond.green_and_lesser()
        row = here.lesser_row(
            [beyond_green, (green_ref[0], green_ref[1])],
            [beyond_lesser, (lesser_ref[0], lesser_ref[1])],
        )
        for to in range(parcel_ref.shape[0]):
            parcel_ref[to, :, 0:size] = row

    operands = [*late, mine, green, lesser, hopping, onsite, parcels]
    return call(
        kernel,
        operands,
        [vmem()] * len(operands),
        jax.ShapeDtypeStruct(parcels.shape, f32),
        input_output_aliases={len(operands) - 1: 0},
    )


def relax(parcels, orbitals, total_energies, grid_total, columns):
    energy_devices, slabs = parcels.shape[:2]
    rows_here = grid_total // energy_devices
    needed, share = grid_share(rows_here, energy_devices)
    rows = -(-needed // SUBLANES) * SUBLANES

    def kernel(parcel_ref, lesser_ref, potential_ref, grid_ref):
        here, slab = lax.axis_index("energy"), lax.axis_index("slab")
        odd = lax.rem(here, 2)
        for parity in range(2):
            both = parcel_ref[here - odd + parity, slab, :, 0 : 2 * orbitals]
            lesser_ref[0, parity : parity + 1, :] = jnp.where(
                odd == parity, both[:, 0:orbitals], both[:, orbitals:]
            )
        empty = jnp.zeros((rows - needed, columns), f32)
        for at in range(slabs):
            for which in range(2):
                if rows > needed:
                    grid_ref[at, which, needed:, :] = empty
            for place in range(2 * needed):
                device, low = place // share, 2 * orbitals + place % share * columns
                row = place % needed
                grid_ref[at, place // needed, row : row + 1, :] = parcel_ref[
                    device, at, :, low : low + columns
                ]
        grid_row = (
            lax.broadcasted_iota(jnp.int32, (rows, columns), 0) + here * rows_here - SWEEPS
        )
        inside = (grid_row >= 0) & (grid_row < grid_total)
        column = lax.broadcasted_iota(jnp.int32, (rows, columns), 1)
        sources, potentials = [], []
        for at in range(slabs):
            both = parcel_ref[0, at, :, 0 : 2 * orbitals]
            for device in range(1, energy_devices):
                both = both + parcel_ref[device, at, :, 0 : 2 * orbitals]
            density = (4.0 / total_energies) * (both[:, 0:orbitals] + both[:, orbitals:])
            index = grid_ref[at, 1].astype(jnp.int32)
            found = jnp.zeros((rows, columns), f32)
            for low in range(0, orbitals, LANES):
                table = jnp.broadcast_to(density[:, low : low + LANES], (rows, LANES))
                within = jnp.clip(index - low, 0, LANES - 1)
                value = jnp.take_along_axis(table, within, axis=1)
                found = jnp.where((index >= low) & (index < low + LANES), value, found)
            sources.append(CHARGE * found)
            potentials.append(grid_ref[at, 0])
        pivots = [MAIN_DIAGONAL]
        for at in range(1, slabs):
            pivots.append(MAIN_DIAGONAL - 1.0 / pivots[-1])
        for sweep in range(SWEEPS):
            eliminated = []
            for at in range(slabs):
                p = potentials[at]
                beside = (
                    pltpu.roll(p, 1, 0)
                    + pltpu.roll(p, rows - 1, 0)
                    + jnp.where(column == 0, 0.0, pltpu.roll(p, 1, 1))
                    + jnp.where(column == columns - 1, 0.0, pltpu.roll(p, columns - 1, 1))
                )
                right = sources[at] + ANISO * beside
                if at:
                    right = right + (1.0 / pivots[at - 1]) * eliminated[-1]
                eliminated.append(right)
            after = None
            for at in reversed(range(slabs)):
                value = eliminated[at] if after is None else eliminated[at] + after
                after = value * (1.0 / pivots[at])
                potentials[at] = jnp.where(inside, after, 0.0)
        for at in range(slabs):
            grid_ref[at, 0] = potentials[at]
        potential_ref[0] = grid_ref[slab, 0, SWEEPS : SWEEPS + rows_here, :]

    return call(
        kernel,
        (parcels,),
        [vmem()],
        [
            jax.ShapeDtypeStruct((1, 2, orbitals), f32),
            jax.ShapeDtypeStruct((1, rows_here, columns), f32),
        ],
        scratch_shapes=[pltpu.VMEM((slabs, 2, rows, columns), f32)],
    )


def per_device(
    onsite, hopping, coupling, boundary_green, damping, occupation, tile_map, prev_potential
):
    energy_devices, slabs = lax.axis_size("energy"), lax.axis_size("slab")
    orbitals = onsite.shape[1]
    assert boundary_green.shape[2] == SHIFT and energy_devices % 2 == 0
    total_energies = SHIFT * energy_devices

    swaps = [
        [pair for i in range(low, slabs - 1, 2) for pair in ((i, i + 1), (i + 1, i))]
        for low in (1, 0)
    ]
    last = energy_devices - 1
    pair = [(i, i ^ 1) for i in range(energy_devices)]
    far = [(i, i + 2) for i in range(1, last, 2) if i + 2 <= last]
    far += [(i, i - 2) for i in range(2, energy_devices, 2)]
    near = [(to, i) for i, to in far]

    common = (hopping, onsite)
    blocks = block_messages(boundary_green, coupling, damping, occupation)
    crossed = [lax.ppermute(part, "energy", pair) for part in blocks[:2]]
    own_sides = [[lax.ppermute(part, "slab", way) for way in swaps] for part in blocks[2:]]
    mine = own_self_energy(*own_sides, coupling, damping, occupation)
    early = lax.ppermute(mine, "energy", far)
    own_green, own_lesser = green_and_lesser([mine], *common, "own", total_energies)
    paired, late = [], []
    for plane, part in enumerate(crossed):
        sides = [lax.ppermute(part, "slab", way) for way in swaps]
        if plane:
            part, own_green = lax.optimization_barrier((part, own_green))
        paired.append(pair_self_energy(sides, coupling, own_sides[0], part))
        late.append(lax.ppermute(paired[-1], "energy", near))
    pair_green, pair_lesser = green_and_lesser(paired, *common, "pair", total_energies)
    parcels = pair_pass(
        early, paired, own_green, own_lesser, *common, tile_map, prev_potential, total_energies
    )
    parcels = own_pass(late, mine, pair_green, pair_lesser, *common, parcels, total_energies)
    parcels = lax.all_to_all(parcels, DEVICES, 0, 0)
    parcels = parcels.reshape(energy_devices, slabs, *parcels.shape[1:])
    return relax(parcels, orbitals, total_energies, *tile_map.shape[1:])


def solution(mesh):
    in_specs = (
        P("slab", None),
        P("slab", None, None),
        P("slab", None),
        P(None, "slab", "energy", None, None),
        P("slab", "energy"),
        P("slab", "energy"),
        P("slab", None, None),
        P("slab", None, None),
    )
    out_specs = (P("slab", "energy", None), P("slab", "energy", None))
    return jax.shard_map(
        per_device, mesh=mesh, in_specs=in_specs, out_specs=out_specs, check_vma=False
    )
```

```python
import functools

import jax
import jax.numpy as jnp
from jax import lax
from jax.experimental import pallas as pl
from jax.experimental.pallas import tpu as pltpu
from jax.sharding import PartitionSpec as P

SHIFT = 2
SWEEPS = 2
PHONON = 0.5
CHARGE = 2.0
ANISO = 0.05
SCREEN = 0.05
MAIN_DIAGONAL = 2.0 + 4.0 * ANISO + SCREEN
LANES = 128
SUBLANES = 8
CROSS_ROWS = 8
VMEM_BYTES = 48 * 1024 * 1024

f32 = jnp.float32
bf16 = jnp.bfloat16
DEVICES = ("energy", "slab")


def parts(matrix):
    high = matrix.astype(bf16)
    return high, (matrix - high.astype(f32)).astype(bf16)


def dot(left, right, transposed=False):
    contract = (((1,), (1 if transposed else 0,)), ((), ()))

    def multiply(a, b):
        return lax.dot_general(a, b, contract, preferred_element_type=f32)

    size = left[0].shape[0]
    both = multiply(jnp.concatenate(left, axis=0), right[0])
    return both[:size] + both[size:] + multiply(left[0], right[1])


def factor(matrix):
    return parts(matrix[0]), parts(matrix[1]), parts(matrix[0] + matrix[1])


def adjoint_factor(matrix):
    return parts(matrix[0]), parts(matrix[1]), parts(matrix[0] - matrix[1])


def product(left, right):
    real, imag, both = (dot(a, b) for a, b in zip(left, right))
    return real - imag, both - real - imag


def adjoint_product(left, right):
    real, imag, both = (dot(a, b, transposed=True) for a, b in zip(left, right))
    return real + imag, both - real + imag


def add(*matrices):
    return sum(m[0] for m in matrices), sum(m[1] for m in matrices)


def as_column(row):
    size = row.shape[1]
    return jnp.broadcast_to(row, (SUBLANES, size)).T[:, 0:1]


def start_of(energy, onsite, damping):
    real = energy - onsite
    modulus = real * real + damping * damping
    present = damping > 0.0
    modulus = jnp.where(present, modulus, 1.0)
    return jnp.where(present, real / modulus, 0.0), jnp.where(present, -damping / modulus, 0.0)


def scale(matrix, factor):
    return (
        matrix[0] * factor[0] - matrix[1] * factor[1],
        matrix[0] * factor[1] + matrix[1] * factor[0],
    )


def invert(coupled, row, column):
    b1 = scale(coupled, row)
    b1_factor = factor(b1)
    b2 = product(b1_factor, b1_factor)
    b2_factor = factor(b2)
    b4 = product(b2_factor, b2_factor)
    b3 = product(b1_factor, b2_factor)
    t = add(b1, b2, b3)
    rest = product(factor(t), factor(b4))
    size = b1[0].shape[0]
    unit = (
        lax.broadcasted_iota(jnp.int32, (size, size), 0)
        == lax.broadcasted_iota(jnp.int32, (size, size), 1)
    ).astype(f32)
    total = add(t, b4, rest)
    return scale((unit + total[0], total[1]), column)


def halves(message_ref):
    height, columns = message_ref.shape
    return message_ref.at[pl.ds(columns, height - columns)], message_ref.at[pl.ds(0, columns)]


class Element:
    def __init__(self, message_refs, hopping_ref, onsite_ref, chain, total_energies):
        size = hopping_ref.shape[-1]
        parity = lax.rem(lax.axis_index("energy"), SHIFT)
        index = (SHIFT * chain + parity).astype(f32)
        energy = -2.0 + (4.0 / total_energies) * (index + 0.5)
        real_ref, imag_ref = message_refs if len(message_refs) == 2 else halves(message_refs[0])
        self.sigma = (real_ref[0:size, :], imag_ref[...])
        damping = real_ref[size : size + 1, :]
        self.occupation = real_ref[size + 1 : size + 2, :]
        onsite = onsite_ref[...]
        self.row = start_of(energy, onsite, damping)
        self.column = tuple(as_column(part) for part in self.row)
        self.hopping = hopping_ref[0]

    def lesser_source(self):
        real, imag = self.sigma
        return -self.occupation * (real - real.T), -self.occupation * (imag + imag.T)

    def green(self, phonon=None):
        coupled = (self.hopping + self.sigma[0], self.sigma[1])
        if phonon is not None:
            coupled = add(coupled, phonon)
        return invert(coupled, self.row, self.column)

    def green_and_lesser(self):
        green = self.green()
        mixed = product(factor(green), factor(self.lesser_source()))
        return green, adjoint_product(factor(mixed), adjoint_factor(green))

    def lesser_row(self, greens, lessers):
        half = tuple(PHONON * part for part in add(*greens))
        green = self.green(half)
        source = add(self.lesser_source(), tuple(PHONON * part for part in add(*lessers)))
        real, imag = parts(green[0]), parts(green[1])
        source_real, source_imag = parts(source[0]), parts(source[1])
        terms = green[0] * dot(real, source_imag) + green[1] * dot(imag, source_imag)
        terms = terms - 2.0 * green[1] * dot(real, source_real)
        column = jnp.sum(terms, axis=1, keepdims=True)
        return jnp.broadcast_to(column, (column.shape[0], LANES)).T[0:1, :]


def chain_places():
    here = lax.axis_index("energy")
    odd = lax.rem(here, 2)
    step = 1 - 2 * odd
    return {"own": here, "pair": here + step, "early": here + 2 * step, "late": here - step}


def vmem():
    return pl.BlockSpec(memory_space=pltpu.VMEM)


def call(kernel, operands, specs, shapes, **options):
    several = isinstance(shapes, list)
    return pl.pallas_call(
        kernel,
        out_shape=shapes,
        in_specs=specs,
        out_specs=[vmem() for _ in shapes] if several else vmem(),
        compiler_params=pltpu.CompilerParams(vmem_limit_bytes=VMEM_BYTES),
        cost_estimate=pl.CostEstimate(flops=0, transcendentals=0, bytes_accessed=0),
        **options,
    )(*operands)


def block_messages(boundary_green, coupling, damping, occupation):
    _, _, _, rows, columns = boundary_green.shape

    def kernel(block_ref, coupling_ref, *refs):
        level_refs, (real_ref, imag_ref), own_refs = refs[:2], refs[2:4], refs[4:6]
        own_levels_ref, held_refs, sems = refs[6], refs[7:9], refs[9]
        parity = lax.rem(lax.axis_index("energy"), SHIFT)
        moves = [
            (block_ref.at[0, 0, 1 - parity], real_ref.at[pl.ds(0, rows)]),
            *zip(level_refs, held_refs),
            (block_ref.at[1, 0, 1 - parity], imag_ref.at[pl.ds(0, rows)]),
            (block_ref.at[0, 0, parity], own_refs[0].at[pl.ds(0, rows)]),
            (coupling_ref, own_refs[0].at[pl.ds(rows, 1)]),
            (block_ref.at[1, 0, parity], own_refs[1]),
        ]
        copies = [
            pltpu.make_async_copy(source, target, sems.at[at])
            for at, (source, target) in enumerate(moves)
        ]
        for copy in copies:
            copy.start()
        for copy in copies:
            copy.wait()
        damping_here, occupation_here = (held_ref[...] for held_ref in held_refs)
        which = lax.broadcasted_iota(jnp.int32, (SUBLANES, columns), 0)
        levels = [
            jnp.where(which == 0, damping_here[:, at : at + 1], occupation_here[:, at : at + 1])
            for at in range(SHIFT)
        ]
        real_ref[rows : rows + SUBLANES, :] = jnp.where(parity == 0, levels[1], levels[0])
        own_levels_ref[...] = jnp.where(parity == 0, levels[0], levels[1])

    operands = (boundary_green, coupling, damping, occupation)
    return call(
        kernel,
        [pltpu.with_memory_space_constraint(x, pltpu.HBM) for x in operands],
        [pl.BlockSpec(memory_space=pltpu.HBM)] * 4,
        [
            jax.ShapeDtypeStruct((height, columns), f32)
            for height in (rows + CROSS_ROWS, rows + CROSS_ROWS, rows + SUBLANES, rows, SUBLANES)
        ],
        scratch_shapes=[
            pltpu.VMEM(damping.shape, f32),
            pltpu.VMEM(damping.shape, f32),
            pltpu.SemaphoreType.DMA((7,)),
        ],
    )


def slab_weights(coupling_ref, side_refs):
    even = lax.rem(lax.axis_index("slab"), 2) == 0
    below = coupling_ref.shape[1]
    weights = []
    for side_ref, before in zip(side_refs, (even, jnp.logical_not(even))):
        row = jnp.where(before, side_ref[below : below + 1, :], coupling_ref[...])
        weights.append(row * as_column(row))
    return weights


def own_self_energy(real_sides, imag_sides, coupling, levels):
    columns = coupling.shape[1]

    def kernel(*refs):
        real_refs, imag_refs = refs[:2], refs[2:4]
        coupling_ref, levels_ref, out_ref = refs[4:]
        weights = slab_weights(coupling_ref, real_refs)
        rows = pl.ds(0, columns)
        for low, side_refs in ((0, imag_refs), (columns, real_refs)):
            outer, inner = (w * ref[rows, :] for w, ref in zip(weights, side_refs))
            out_ref[pl.ds(low, columns), :] = outer + inner
        out_ref[2 * columns :, :] = levels_ref[...]

    return call(
        kernel,
        (*real_sides, *imag_sides, coupling, levels),
        [vmem()] * 6,
        jax.ShapeDtypeStruct((2 * columns + SUBLANES, columns), f32),
    )


def pair_self_energy(sides, coupling, own_sides, crossed, extra):
    columns = crossed.shape[1]
    height = columns + extra

    def kernel(outer_ref, inner_ref, coupling_ref, own_outer_ref, own_inner_ref, crossed_ref, out_ref):
        outer_weight, inner_weight = slab_weights(coupling_ref, (own_outer_ref, own_inner_ref))
        rows = pl.ds(0, columns)
        out_ref[rows, :] = outer_weight * outer_ref[rows, :] + inner_weight * inner_ref[rows, :]
        if extra:
            out_ref[columns:, :] = crossed_ref[columns:height, :]

    operands = (*sides, coupling, *own_sides, crossed)
    return call(kernel, operands, [vmem()] * 6, jax.ShapeDtypeStruct((height, columns), f32))


def green_and_lesser(message, hopping, onsite, place, total_energies):
    count = len(message)

    def kernel(*refs):
        hopping_ref, onsite_ref, green_ref, lesser_ref = refs[count:]
        element = Element(
            refs[:count], hopping_ref, onsite_ref, chain_places()[place], total_energies
        )
        green, lesser = element.green_and_lesser()
        for plane in range(2):
            green_ref[plane] = green[plane]
            lesser_ref[plane] = lesser[plane]

    size = hopping.shape[-1]
    shape = jax.ShapeDtypeStruct((2, size, size), f32)
    operands = (*message, hopping, onsite)
    return call(kernel, operands, [vmem()] * len(operands), [shape, shape])


def grid_share(rows_here, energy_devices):
    needed = rows_here + 2 * SWEEPS
    return needed, -(-2 * needed // energy_devices)


def pair_pass(early, paired, green, lesser, hopping, onsite, tile_map, potential, total_energies):
    size = hopping.shape[-1]
    energy_devices, slabs = lax.axis_size("energy"), lax.axis_size("slab")
    grid_total, columns = tile_map.shape[1:]
    rows_here = grid_total // energy_devices
    needed, share = grid_share(rows_here, energy_devices)
    rows = -(-needed // SUBLANES) * SUBLANES
    padded = grid_total + SUBLANES
    length = max(share * columns, size)

    def kernel(*refs):
        early_refs, paired_refs, refs = refs[:1], refs[1:3], refs[3:]
        green_ref, lesser_ref, hopping_ref, onsite_ref, tile_ref, potential_ref = refs[:6]
        parcel_ref, row_ref, local_ref, grid_ref = refs[6:]
        chains = chain_places()
        here = Element(paired_refs, hopping_ref, onsite_ref, chains["pair"], total_energies)
        beyond = Element(early_refs, hopping_ref, onsite_ref, chains["early"], total_energies)
        beyond_green, beyond_lesser = beyond.green_and_lesser()
        row = here.lesser_row(
            [beyond_green, (green_ref[0], green_ref[1])],
            [beyond_lesser, (lesser_ref[0], lesser_ref[1])],
        )
        row_ref[...] = row
        at_energy, at_slab = lax.axis_index("energy"), lax.axis_index("slab")
        border = jnp.zeros((SUBLANES, columns), f32)
        for at, plane in enumerate((potential_ref[0], tile_ref[0].astype(f32))):
            low = at * padded
            grid_ref[low : low + SUBLANES, :] = border
            grid_ref[low + padded - SUBLANES : low + padded, :] = border
            grid_ref[low + SWEEPS : low + SWEEPS + grid_total, :] = plane
        for at in range(2):
            low = pl.multiple_of(at * padded + at_energy * rows_here, SUBLANES)
            local_ref[at] = grid_ref[pl.ds(low, rows), :]
        first = at_energy * share

        def filled(pieces):
            piece = jnp.concatenate(pieces, axis=1)
            short = length - piece.shape[1]
            if short:
                piece = jnp.concatenate([piece, jnp.zeros((1, short), f32)], axis=1)
            return piece

        same = filled([row])
        for to in range(energy_devices):
            pieces = []
            for i in range(share):
                place = jnp.minimum(first + i, 2 * needed - 1)
                which = (place >= needed).astype(jnp.int32)
                source = which * (padded - needed) + place + to * rows_here
                pieces.append(grid_ref[pl.ds(source, 1), :])
            other = filled(pieces)
            for slab in range(slabs):
                parcel_ref[to * slabs + slab, :, size:] = jnp.where(at_slab == slab, same, other)

    operands = [early, *paired, green, lesser, hopping, onsite, tile_map, potential]
    return call(
        kernel,
        operands,
        [vmem()] * len(operands),
        [
            jax.ShapeDtypeStruct((energy_devices * slabs, 1, size + length), f32),
            jax.ShapeDtypeStruct((1, size), f32),
            jax.ShapeDtypeStruct((2, rows, columns), f32),
        ],
        scratch_shapes=[pltpu.VMEM((2 * padded, columns), f32)],
    )


def own_pass(late, mine, green, lesser, hopping, onsite, parcels, other_row, total_energies):
    size = hopping.shape[-1]

    def kernel(*refs):
        late_refs, mine_refs, refs = refs[:2], refs[2:3], refs[3:]
        green_ref, lesser_ref, hopping_ref, onsite_ref, other_ref, _, parcel_ref, row_ref = refs
        chains = chain_places()
        here = Element(mine_refs, hopping_ref, onsite_ref, chains["own"], total_energies)
        beyond = Element(late_refs, hopping_ref, onsite_ref, chains["late"], total_energies)
        beyond_green, beyond_lesser = beyond.green_and_lesser()
        row = here.lesser_row(
            [beyond_green, (green_ref[0], green_ref[1])],
            [beyond_lesser, (lesser_ref[0], lesser_ref[1])],
        )
        row_ref[...] = row
        both = row + other_ref[...]
        for to in range(parcel_ref.shape[0]):
            parcel_ref[to, :, 0:size] = both

    operands = [*late, mine, green, lesser, hopping, onsite, other_row, parcels]
    return call(
        kernel,
        operands,
        [vmem()] * len(operands),
        [
            jax.ShapeDtypeStruct(parcels.shape, f32),
            jax.ShapeDtypeStruct(other_row.shape, f32),
        ],
        input_output_aliases={len(operands) - 1: 0},
    )


def relax(parcels, own_row, local, orbitals, total_energies, grid_total, columns):
    energy_devices, slabs = parcels.shape[:2]
    rows_here = grid_total // energy_devices
    needed, share = grid_share(rows_here, energy_devices)
    rows = local.shape[1]

    def kernel(parcel_ref, own_ref, local_ref, lesser_ref, potential_ref, grid_ref):
        here, slab = lax.axis_index("energy"), lax.axis_index("slab")
        odd = lax.rem(here, 2)
        pair_row = parcel_ref[here + 1 - 2 * odd, slab, :, orbitals : 2 * orbitals]
        for parity in range(2):
            lesser_ref[0, parity : parity + 1, :] = jnp.where(
                odd == parity, own_ref[...], pair_row
            )
        empty = jnp.zeros((rows - needed, columns), f32)
        for at in range(slabs):
            for which in range(2):
                if rows > needed:
                    grid_ref[at, which, needed:, :] = empty
            for place in range(2 * needed):
                device, low = place // share, orbitals + place % share * columns
                row = place % needed
                grid_ref[at, place // needed, row : row + 1, :] = parcel_ref[
                    device, at, :, low : low + columns
                ]
        grid_ref[slab] = local_ref[...]
        grid_row = (
            lax.broadcasted_iota(jnp.int32, (rows, columns), 0) + here * rows_here - SWEEPS
        )
        inside = (grid_row >= 0) & (grid_row < grid_total)
        column = lax.broadcasted_iota(jnp.int32, (rows, columns), 1)
        sources, potentials = [], []
        for at in range(slabs):
            total = parcel_ref[0, at, :, 0:orbitals]
            for device in range(1, energy_devices):
                total = total + parcel_ref[device, at, :, 0:orbitals]
            density = (4.0 / total_energies) * total
            index = grid_ref[at, 1].astype(jnp.int32)
            found = jnp.zeros((rows, columns), f32)
            for low in range(0, orbitals, LANES):
                table = jnp.broadcast_to(density[:, low : low + LANES], (rows, LANES))
                within = jnp.clip(index - low, 0, LANES - 1)
                value = jnp.take_along_axis(table, within, axis=1)
                found = jnp.where((index >= low) & (index < low + LANES), value, found)
            sources.append(CHARGE * found)
            potentials.append(grid_ref[at, 0])
        pivots = [MAIN_DIAGONAL]
        for at in range(1, slabs):
            pivots.append(MAIN_DIAGONAL - 1.0 / pivots[-1])
        for sweep in range(SWEEPS):
            eliminated = []
            for at in range(slabs):
                p = potentials[at]
                beside = (
                    pltpu.roll(p, 1, 0)
                    + pltpu.roll(p, rows - 1, 0)
                    + jnp.where(column == 0, 0.0, pltpu.roll(p, 1, 1))
                    + jnp.where(column == columns - 1, 0.0, pltpu.roll(p, columns - 1, 1))
                )
                right = sources[at] + ANISO * beside
                if at:
                    right = right + (1.0 / pivots[at - 1]) * eliminated[-1]
                eliminated.append(right)
            after = None
            for at in reversed(range(slabs)):
                value = eliminated[at] if after is None else eliminated[at] + after
                after = value * (1.0 / pivots[at])
                potentials[at] = jnp.where(inside, after, 0.0)
        for at in range(slabs):
            grid_ref[at, 0] = potentials[at]
        potential_ref[0] = grid_ref[slab, 0, SWEEPS : SWEEPS + rows_here, :]

    return call(
        kernel,
        (parcels, own_row, local),
        [vmem()] * 3,
        [
            jax.ShapeDtypeStruct((1, 2, orbitals), f32),
            jax.ShapeDtypeStruct((1, rows_here, columns), f32),
        ],
        scratch_shapes=[pltpu.VMEM((slabs, 2, rows, columns), f32)],
    )


def per_device(
    onsite, hopping, coupling, boundary_green, damping, occupation, tile_map, prev_potential
):
    energy_devices, slabs = lax.axis_size("energy"), lax.axis_size("slab")
    orbitals = onsite.shape[1]
    assert boundary_green.shape[2] == SHIFT and energy_devices % 2 == 0
    total_energies = SHIFT * energy_devices

    swaps = [
        [pair for i in range(low, slabs - 1, 2) for pair in ((i, i + 1), (i + 1, i))]
        for low in (1, 0)
    ]
    last = energy_devices - 1
    pair = [(i, i ^ 1) for i in range(energy_devices)]
    far = [(i, i + 2) for i in range(1, last, 2) if i + 2 <= last]
    far += [(i, i - 2) for i in range(2, energy_devices, 2)]
    near = [(to, i) for i, to in far]

    common = (hopping, onsite)
    blocks = block_messages(boundary_green, coupling, damping, occupation)
    crossed = [lax.ppermute(part, "energy", pair) for part in blocks[:2]]
    own_sides = [[lax.ppermute(part, "slab", way) for way in swaps] for part in blocks[2:4]]
    mine = own_self_energy(*own_sides, coupling, blocks[4])
    early = lax.ppermute(mine, "energy", far)
    own_green, own_lesser = green_and_lesser([mine], *common, "own", total_energies)
    paired, late = [], []
    for plane, part in enumerate(crossed):
        sides = [lax.ppermute(part, "slab", way) for way in swaps]
        if plane:
            part, own_green = lax.optimization_barrier((part, own_green))
        extra = 0 if plane else SUBLANES
        paired.append(pair_self_energy(sides, coupling, own_sides[0], part, extra))
        late.append(lax.ppermute(paired[-1], "energy", near))
    pair_green, pair_lesser = green_and_lesser(paired, *common, "pair", total_energies)
    parcels, pair_row, local = pair_pass(
        early, paired, own_green, own_lesser, *common, tile_map, prev_potential, total_energies
    )
    parcels, own_row = own_pass(
        late, mine, pair_green, pair_lesser, *common, parcels, pair_row, total_energies
    )
    parcels = lax.all_to_all(parcels, DEVICES, 0, 0)
    parcels = parcels.reshape(energy_devices, slabs, *parcels.shape[1:])
    return relax(parcels, own_row, local, orbitals, total_energies, *tile_map.shape[1:])


def solution(mesh):
    in_specs = (
        P("slab", None),
        P("slab", None, None),
        P("slab", None),
        P(None, "slab", "energy", None, None),
        P("slab", "energy"),
        P("slab", "energy"),
        P("slab", None, None),
        P("slab", None, None),
    )
    out_specs = (P("slab", "energy", None), P("slab", "energy", None))
    return jax.shard_map(
        per_device, mesh=mesh, in_specs=in_specs, out_specs=out_specs, check_vma=False
    )
```

```python
import functools

import jax
import jax.numpy as jnp
from jax import lax
from jax.experimental import pallas as pl
from jax.experimental.pallas import tpu as pltpu
from jax.sharding import PartitionSpec as P

SHIFT = 2
SWEEPS = 2
PHONON = 0.5
CHARGE = 2.0
ANISO = 0.05
SCREEN = 0.05
MAIN_DIAGONAL = 2.0 + 4.0 * ANISO + SCREEN
LANES = 128
SUBLANES = 8
BELOW = (8, 0, 16, 16)
VMEM_BYTES = 48 * 1024 * 1024

f32 = jnp.float32
bf16 = jnp.bfloat16
DEVICES = ("energy", "slab")


def parts(matrix):
    high = matrix.astype(bf16)
    return high, (matrix - high.astype(f32)).astype(bf16)


def dot(left, right, transposed=False):
    contract = (((1,), (1 if transposed else 0,)), ((), ()))

    def multiply(a, b):
        return lax.dot_general(a, b, contract, preferred_element_type=f32)

    size = left[0].shape[0]
    both = multiply(jnp.concatenate(left, axis=0), right[0])
    return both[:size] + both[size:] + multiply(left[0], right[1])


def factor(matrix):
    return parts(matrix[0]), parts(matrix[1]), parts(matrix[0] + matrix[1])


def adjoint_factor(matrix):
    return parts(matrix[0]), parts(matrix[1]), parts(matrix[0] - matrix[1])


def product(left, right):
    real, imag, both = (dot(a, b) for a, b in zip(left, right))
    return real - imag, both - real - imag


def adjoint_product(left, right):
    real, imag, both = (dot(a, b, transposed=True) for a, b in zip(left, right))
    return real + imag, both - real + imag


def add(*matrices):
    return sum(m[0] for m in matrices), sum(m[1] for m in matrices)


def as_column(row):
    size = row.shape[1]
    return jnp.broadcast_to(row, (SUBLANES, size)).T[:, 0:1]


def start_of(energy, onsite, damping):
    real = energy - onsite
    modulus = real * real + damping * damping
    present = damping > 0.0
    modulus = jnp.where(present, modulus, 1.0)
    return jnp.where(present, real / modulus, 0.0), jnp.where(present, -damping / modulus, 0.0)


def scale(matrix, factor):
    return (
        matrix[0] * factor[0] - matrix[1] * factor[1],
        matrix[0] * factor[1] + matrix[1] * factor[0],
    )


def invert(coupled, row, column, between=()):
    given = None
    steps = iter(between)

    def beside():
        nonlocal given
        step = next(steps, None)
        if step is not None:
            given = step(given)

    b1 = scale(coupled, row)
    b1_factor = factor(b1)
    b2 = product(b1_factor, b1_factor)
    beside()
    b2_factor = factor(b2)
    b4 = product(b2_factor, b2_factor)
    b3 = product(b1_factor, b2_factor)
    beside()
    t = add(b1, b2, b3)
    rest = product(factor(t), factor(b4))
    size = b1[0].shape[0]
    unit = (
        lax.broadcasted_iota(jnp.int32, (size, size), 0)
        == lax.broadcasted_iota(jnp.int32, (size, size), 1)
    ).astype(f32)
    total = add(t, b4, rest)
    return scale((unit + total[0], total[1]), column), given


def halves(message_ref):
    height, columns = message_ref.shape
    return message_ref.at[pl.ds(columns, height - columns)], message_ref.at[pl.ds(0, columns)]


class Element:
    def __init__(self, message_refs, hopping_ref, onsite_ref, chain, total_energies):
        size = hopping_ref.shape[-1]
        parity = lax.rem(lax.axis_index("energy"), SHIFT)
        index = (SHIFT * chain + parity).astype(f32)
        energy = -2.0 + (4.0 / total_energies) * (index + 0.5)
        self.real_ref, self.imag_ref = (
            message_refs if len(message_refs) == 2 else halves(message_refs[0])
        )
        damping = self.real_ref[size : size + 1, :]
        self.occupation = self.real_ref[size + 1 : size + 2, :]
        onsite = onsite_ref[...]
        self.row = start_of(energy, onsite, damping)
        self.column = tuple(as_column(part) for part in self.row)
        self.hopping_ref = hopping_ref

    def sigma(self):
        size = self.hopping_ref.shape[-1]
        return self.real_ref[0:size, :], self.imag_ref[0:size, :]

    def coupled(self):
        real, imag = self.sigma()
        return self.hopping_ref[0] + real, imag

    def source(self):
        real, imag = self.sigma()
        return -self.occupation * (real - real.T), -self.occupation * (imag + imag.T)

    def green(self):
        return invert(self.coupled(), self.row, self.column)[0]

    def green_and_lesser(self, source):
        green = self.green()
        mixed = product(factor(green), factor(source))
        return green, adjoint_product(factor(mixed), adjoint_factor(green))

    def lesser_row(self, coupled, source, beyond):
        beyond_source = factor(beyond.source())
        beyond_green = beyond.green()
        steps = (
            lambda _: product(factor(beyond_green), beyond_source),
            lambda mixed: adjoint_product(factor(mixed), adjoint_factor(beyond_green)),
        )
        coupled = with_half(coupled, beyond_green)
        green, lesser = invert(coupled, self.row, self.column, steps)
        source = with_half(source, lesser)
        real, imag = parts(green[0]), parts(green[1])
        source_real, source_imag = parts(source[0]), parts(source[1])
        terms = green[0] * dot(real, source_imag) + green[1] * dot(imag, source_imag)
        terms = terms - 2.0 * green[1] * dot(real, source_real)
        column = jnp.sum(terms, axis=1, keepdims=True)
        return jnp.broadcast_to(column, (column.shape[0], LANES)).T[0:1, :]


def with_half(matrix, phonon):
    return tuple(a + PHONON * b for a, b in zip(matrix, phonon))


def load(ref):
    return ref[0], ref[1]


def store(ref, matrix):
    ref[0], ref[1] = matrix


def chain_places():
    here = lax.axis_index("energy")
    odd = lax.rem(here, 2)
    step = 1 - 2 * odd
    return {"own": here, "pair": here + step, "early": here + 2 * step, "late": here - step}


def vmem():
    return pl.BlockSpec(memory_space=pltpu.VMEM)


def call(kernel, operands, specs, shapes, **options):
    several = isinstance(shapes, list)
    return pl.pallas_call(
        kernel,
        out_shape=shapes,
        in_specs=specs,
        out_specs=[vmem() for _ in shapes] if several else vmem(),
        compiler_params=pltpu.CompilerParams(vmem_limit_bytes=VMEM_BYTES),
        cost_estimate=pl.CostEstimate(flops=0, transcendentals=0, bytes_accessed=0),
        **options,
    )(*operands)


def block_messages(boundary_green, coupling, damping, occupation):
    _, _, _, rows, columns = boundary_green.shape

    def kernel(block_ref, coupling_ref, *refs):
        level_refs, (real_ref, imag_ref), own_refs = refs[:2], refs[2:4], refs[4:6]
        own_levels_ref, held_refs, sems = refs[6], refs[7:9], refs[9]
        parity = lax.rem(lax.axis_index("energy"), SHIFT)
        moves = [
            (block_ref.at[0, 0, 1 - parity], real_ref.at[pl.ds(0, rows)]),
            *zip(level_refs, held_refs),
            (block_ref.at[1, 0, 1 - parity], imag_ref.at[pl.ds(0, rows)]),
            (block_ref.at[0, 0, parity], own_refs[0].at[pl.ds(0, rows)]),
            (coupling_ref, own_refs[0].at[pl.ds(rows, 1)]),
            (block_ref.at[1, 0, parity], own_refs[1].at[pl.ds(0, rows)]),
        ]
        copies = [
            pltpu.make_async_copy(source, target, sems.at[at])
            for at, (source, target) in enumerate(moves)
        ]
        for copy in copies:
            copy.start()
        for copy in copies:
            copy.wait()
        damping_here, occupation_here = (held_ref[...] for held_ref in held_refs)
        which = lax.broadcasted_iota(jnp.int32, (SUBLANES, columns), 0)
        levels = [
            jnp.where(which == 0, damping_here[:, at : at + 1], occupation_here[:, at : at + 1])
            for at in range(SHIFT)
        ]
        real_ref[rows : rows + SUBLANES, :] = jnp.where(parity == 0, levels[1], levels[0])
        own_levels_ref[...] = jnp.where(parity == 0, levels[0], levels[1])

    operands = (boundary_green, coupling, damping, occupation)
    return call(
        kernel,
        [pltpu.with_memory_space_constraint(x, pltpu.HBM) for x in operands],
        [pl.BlockSpec(memory_space=pltpu.HBM)] * 4,
        [
            jax.ShapeDtypeStruct((height, columns), f32)
            for height in (*(rows + extra for extra in BELOW), SUBLANES)
        ],
        scratch_shapes=[
            pltpu.VMEM(damping.shape, f32),
            pltpu.VMEM(damping.shape, f32),
            pltpu.SemaphoreType.DMA((7,)),
        ],
    )


def slab_weights(coupling_ref, side_refs):
    even = lax.rem(lax.axis_index("slab"), 2) == 0
    below = coupling_ref.shape[1]
    weights = []
    for side_ref, before in zip(side_refs, (even, jnp.logical_not(even))):
        row = jnp.where(before, side_ref[below : below + 1, :], coupling_ref[...])
        weights.append(row * as_column(row))
    return weights


def own_self_energy(real_sides, imag_sides, coupling, levels):
    columns = coupling.shape[1]

    def kernel(*refs):
        real_refs, imag_refs = refs[:2], refs[2:4]
        coupling_ref, levels_ref, out_ref = refs[4:]
        weights = slab_weights(coupling_ref, real_refs)
        rows = pl.ds(0, columns)
        for low, side_refs in ((0, imag_refs), (columns, real_refs)):
            outer, inner = (w * ref[rows, :] for w, ref in zip(weights, side_refs))
            out_ref[pl.ds(low, columns), :] = outer + inner
        out_ref[2 * columns :, :] = levels_ref[...]

    return call(
        kernel,
        (*real_sides, *imag_sides, coupling, levels),
        [vmem()] * 6,
        jax.ShapeDtypeStruct((2 * columns + SUBLANES, columns), f32),
    )


def pair_self_energy(sides, coupling, own_sides, crossed, extra):
    columns = crossed.shape[1]
    height = columns + extra

    def kernel(outer_ref, inner_ref, coupling_ref, own_outer_ref, own_inner_ref, crossed_ref, out_ref):
        outer_weight, inner_weight = slab_weights(coupling_ref, (own_outer_ref, own_inner_ref))
        rows = pl.ds(0, columns)
        out_ref[rows, :] = outer_weight * outer_ref[rows, :] + inner_weight * inner_ref[rows, :]
        if extra:
            out_ref[columns:, :] = crossed_ref[columns:height, :]

    operands = (*sides, coupling, *own_sides, crossed)
    return call(kernel, operands, [vmem()] * 6, jax.ShapeDtypeStruct((height, columns), f32))


def own_first(message, hopping, onsite, total_energies):
    def kernel(message_ref, hopping_ref, onsite_ref, green_ref, lesser_ref, source_ref):
        place = chain_places()["own"]
        element = Element([message_ref], hopping_ref, onsite_ref, place, total_energies)
        source = element.source()
        green, lesser = element.green_and_lesser(source)
        for ref, matrix in ((green_ref, green), (lesser_ref, lesser), (source_ref, source)):
            store(ref, matrix)

    size = hopping.shape[-1]
    shape = jax.ShapeDtypeStruct((2, size, size), f32)
    return call(kernel, (message, hopping, onsite), [vmem()] * 3, [shape] * 3)


def pair_first(paired, mine, green, lesser, source, hopping, onsite, total_energies):
    def kernel(*refs):
        paired_refs, mine_refs, (green_ref, lesser_ref, source_ref) = refs[:2], refs[2:3], refs[3:6]
        hopping_ref, onsite_ref, *out_refs = refs[6:]
        chains = chain_places()
        pair = Element(paired_refs, hopping_ref, onsite_ref, chains["pair"], total_energies)
        own = Element(mine_refs, hopping_ref, onsite_ref, chains["own"], total_energies)
        pair_source = pair.source()
        store(out_refs[0], with_half(pair.coupled(), load(green_ref)))
        store(out_refs[1], with_half(pair_source, load(lesser_ref)))
        pair_green, pair_lesser = pair.green_and_lesser(pair_source)
        store(out_refs[2], with_half(own.coupled(), pair_green))
        store(out_refs[3], with_half(load(source_ref), pair_lesser))

    operands = (*paired, mine, green, lesser, source, hopping, onsite)
    size = hopping.shape[-1]
    shape = jax.ShapeDtypeStruct((2, size, size), f32)
    return call(kernel, operands, [vmem()] * len(operands), [shape] * 4)


def grid_share(rows_here, energy_devices):
    needed = rows_here + 2 * SWEEPS
    return needed, -(-2 * needed // energy_devices)


def pair_pass(early, paired, coupled, source, hopping, onsite, tile_map, potential, total_energies):
    size = hopping.shape[-1]
    energy_devices, slabs = lax.axis_size("energy"), lax.axis_size("slab")
    grid_total, columns = tile_map.shape[1:]
    rows_here = grid_total // energy_devices
    needed, share = grid_share(rows_here, energy_devices)
    rows = -(-needed // SUBLANES) * SUBLANES
    padded = grid_total + SUBLANES
    length = max(share * columns, size)

    def kernel(*refs):
        early_refs, paired_refs, refs = refs[:1], refs[1:3], refs[3:]
        coupled_ref, source_ref, hopping_ref, onsite_ref, tile_ref, potential_ref = refs[:6]
        parcel_ref, row_ref, local_ref, grid_ref = refs[6:]
        chains = chain_places()
        here = Element(paired_refs, hopping_ref, onsite_ref, chains["pair"], total_energies)
        beyond = Element(early_refs, hopping_ref, onsite_ref, chains["early"], total_energies)
        row = here.lesser_row(load(coupled_ref), load(source_ref), beyond)
        row_ref[...] = row
        at_energy, at_slab = lax.axis_index("energy"), lax.axis_index("slab")
        border = jnp.zeros((SUBLANES, columns), f32)
        for at, plane in enumerate((potential_ref[0], tile_ref[0].astype(f32))):
            low = at * padded
            grid_ref[low : low + SUBLANES, :] = border
            grid_ref[low + padded - SUBLANES : low + padded, :] = border
            grid_ref[low + SWEEPS : low + SWEEPS + grid_total, :] = plane
        for at in range(2):
            low = pl.multiple_of(at * padded + at_energy * rows_here, SUBLANES)
            local_ref[at] = grid_ref[pl.ds(low, rows), :]
        first = at_energy * share

        def filled(pieces):
            piece = jnp.concatenate(pieces, axis=1)
            short = length - piece.shape[1]
            if short:
                piece = jnp.concatenate([piece, jnp.zeros((1, short), f32)], axis=1)
            return piece

        same = filled([row])
        for to in range(energy_devices):
            pieces = []
            for i in range(share):
                place = jnp.minimum(first + i, 2 * needed - 1)
                which = (place >= needed).astype(jnp.int32)
                source = which * (padded - needed) + place + to * rows_here
                pieces.append(grid_ref[pl.ds(source, 1), :])
            other = filled(pieces)
            for slab in range(slabs):
                parcel_ref[to * slabs + slab, :, size:] = jnp.where(at_slab == slab, same, other)

    operands = [early, *paired, coupled, source, hopping, onsite, tile_map, potential]
    return call(
        kernel,
        operands,
        [vmem()] * len(operands),
        [
            jax.ShapeDtypeStruct((energy_devices * slabs, 1, size + length), f32),
            jax.ShapeDtypeStruct((1, size), f32),
            jax.ShapeDtypeStruct((2, rows, columns), f32),
        ],
        scratch_shapes=[pltpu.VMEM((2 * padded, columns), f32)],
    )


def own_pass(late, mine, coupled, source, hopping, onsite, parcels, other_row, total_energies):
    size = hopping.shape[-1]

    def kernel(*refs):
        late_refs, mine_refs, refs = refs[:2], refs[2:3], refs[3:]
        coupled_ref, source_ref, hopping_ref, onsite_ref, other_ref, _, parcel_ref, row_ref = refs
        chains = chain_places()
        here = Element(mine_refs, hopping_ref, onsite_ref, chains["own"], total_energies)
        beyond = Element(late_refs, hopping_ref, onsite_ref, chains["late"], total_energies)
        row = here.lesser_row(load(coupled_ref), load(source_ref), beyond)
        row_ref[...] = row
        both = row + other_ref[...]
        for to in range(parcel_ref.shape[0]):
            parcel_ref[to, :, 0:size] = both

    operands = [*late, mine, coupled, source, hopping, onsite, other_row, parcels]
    return call(
        kernel,
        operands,
        [vmem()] * len(operands),
        [
            jax.ShapeDtypeStruct(parcels.shape, f32),
            jax.ShapeDtypeStruct(other_row.shape, f32),
        ],
        input_output_aliases={len(operands) - 1: 0},
    )


def relax(parcels, own_row, local, orbitals, total_energies, grid_total, columns):
    energy_devices, slabs = parcels.shape[:2]
    rows_here = grid_total // energy_devices
    needed, share = grid_share(rows_here, energy_devices)
    rows = local.shape[1]

    def kernel(parcel_ref, own_ref, local_ref, lesser_ref, potential_ref, grid_ref):
        here, slab = lax.axis_index("energy"), lax.axis_index("slab")
        odd = lax.rem(here, 2)
        pair_row = parcel_ref[here + 1 - 2 * odd, slab, :, orbitals : 2 * orbitals]
        for parity in range(2):
            lesser_ref[0, parity : parity + 1, :] = jnp.where(
                odd == parity, own_ref[...], pair_row
            )
        empty = jnp.zeros((rows - needed, columns), f32)
        for at in range(slabs):
            for which in range(2):
                if rows > needed:
                    grid_ref[at, which, needed:, :] = empty
            for place in range(2 * needed):
                device, low = place // share, orbitals + place % share * columns
                row = place % needed
                grid_ref[at, place // needed, row : row + 1, :] = parcel_ref[
                    device, at, :, low : low + columns
                ]
        grid_ref[slab] = local_ref[...]
        grid_row = (
            lax.broadcasted_iota(jnp.int32, (rows, columns), 0) + here * rows_here - SWEEPS
        )
        inside = (grid_row >= 0) & (grid_row < grid_total)
        column = lax.broadcasted_iota(jnp.int32, (rows, columns), 1)
        sources, potentials = [], []
        for at in range(slabs):
            total = parcel_ref[0, at, :, 0:orbitals]
            for device in range(1, energy_devices):
                total = total + parcel_ref[device, at, :, 0:orbitals]
            density = (4.0 / total_energies) * total
            index = grid_ref[at, 1].astype(jnp.int32)
            found = jnp.zeros((rows, columns), f32)
            for low in range(0, orbitals, LANES):
                table = jnp.broadcast_to(density[:, low : low + LANES], (rows, LANES))
                within = jnp.clip(index - low, 0, LANES - 1)
                value = jnp.take_along_axis(table, within, axis=1)
                found = jnp.where((index >= low) & (index < low + LANES), value, found)
            sources.append(CHARGE * found)
            potentials.append(grid_ref[at, 0])
        pivots = [MAIN_DIAGONAL]
        for at in range(1, slabs):
            pivots.append(MAIN_DIAGONAL - 1.0 / pivots[-1])
        for sweep in range(SWEEPS):
            eliminated = []
            for at in range(slabs):
                p = potentials[at]
                beside = (
                    pltpu.roll(p, 1, 0)
                    + pltpu.roll(p, rows - 1, 0)
                    + jnp.where(column == 0, 0.0, pltpu.roll(p, 1, 1))
                    + jnp.where(column == columns - 1, 0.0, pltpu.roll(p, columns - 1, 1))
                )
                right = sources[at] + ANISO * beside
                if at:
                    right = right + (1.0 / pivots[at - 1]) * eliminated[-1]
                eliminated.append(right)
            after = None
            for at in reversed(range(slabs)):
                value = eliminated[at] if after is None else eliminated[at] + after
                after = value * (1.0 / pivots[at])
                potentials[at] = jnp.where(inside, after, 0.0)
        for at in range(slabs):
            grid_ref[at, 0] = potentials[at]
        potential_ref[0] = grid_ref[slab, 0, SWEEPS : SWEEPS + rows_here, :]

    return call(
        kernel,
        (parcels, own_row, local),
        [vmem()] * 3,
        [
            jax.ShapeDtypeStruct((1, 2, orbitals), f32),
            jax.ShapeDtypeStruct((1, rows_here, columns), f32),
        ],
        scratch_shapes=[pltpu.VMEM((slabs, 2, rows, columns), f32)],
    )


def per_device(
    onsite, hopping, coupling, boundary_green, damping, occupation, tile_map, prev_potential
):
    energy_devices, slabs = lax.axis_size("energy"), lax.axis_size("slab")
    orbitals = onsite.shape[1]
    assert boundary_green.shape[2] == SHIFT and energy_devices % 2 == 0
    total_energies = SHIFT * energy_devices

    swaps = [
        [pair for i in range(low, slabs - 1, 2) for pair in ((i, i + 1), (i + 1, i))]
        for low in (1, 0)
    ]
    last = energy_devices - 1
    pair = [(i, i ^ 1) for i in range(energy_devices)]
    far = [(i, i + 2) for i in range(1, last, 2) if i + 2 <= last]
    far += [(i, i - 2) for i in range(2, energy_devices, 2)]
    near = [(to, i) for i, to in far]

    common = (hopping, onsite)
    blocks = block_messages(boundary_green, coupling, damping, occupation)
    crossed = [lax.ppermute(part, "energy", pair) for part in blocks[:2]]
    own_sides = [[lax.ppermute(part, "slab", way) for way in swaps] for part in blocks[2:4]]
    mine = own_self_energy(*own_sides, coupling, blocks[4])
    early = lax.ppermute(mine, "energy", far)
    own_green, own_lesser, own_source = own_first(mine, *common, total_energies)
    paired, late = [], []
    for plane, part in enumerate(crossed):
        sides = [lax.ppermute(part, "slab", way) for way in swaps]
        if plane:
            part, own_green = lax.optimization_barrier((part, own_green))
        extra = 0 if plane else SUBLANES
        paired.append(pair_self_energy(sides, coupling, own_sides[0], part, extra))
        late.append(lax.ppermute(paired[-1], "energy", near))
    *pair_parts, own_coupled, own_total = pair_first(
        paired, mine, own_green, own_lesser, own_source, *common, total_energies
    )
    parcels, pair_row, local = pair_pass(
        early, paired, *pair_parts, *common, tile_map, prev_potential, total_energies
    )
    parcels, own_row = own_pass(
        late, mine, own_coupled, own_total, *common, parcels, pair_row, total_energies
    )
    parcels = lax.all_to_all(parcels, DEVICES, 0, 0)
    parcels = parcels.reshape(energy_devices, slabs, *parcels.shape[1:])
    return relax(parcels, own_row, local, orbitals, total_energies, *tile_map.shape[1:])


def solution(mesh):
    in_specs = (
        P("slab", None),
        P("slab", None, None),
        P("slab", None),
        P(None, "slab", "energy", None, None),
        P("slab", "energy"),
        P("slab", "energy"),
        P("slab", None, None),
        P("slab", None, None),
    )
    out_specs = (P("slab", "energy", None), P("slab", "energy", None))
    return jax.shard_map(
        per_device, mesh=mesh, in_specs=in_specs, out_specs=out_specs, check_vma=False
    )
```

```python
import functools

import jax
import jax.numpy as jnp
from jax import lax
from jax.experimental import pallas as pl
from jax.experimental.pallas import tpu as pltpu
from jax.sharding import PartitionSpec as P

SHIFT = 2
SWEEPS = 2
PHONON = 0.5
CHARGE = 2.0
ANISO = 0.05
SCREEN = 0.05
MAIN_DIAGONAL = 2.0 + 4.0 * ANISO + SCREEN
LANES = 128
SUBLANES = 8
BELOW = (8, 0, 16, 16)
VMEM_BYTES = 48 * 1024 * 1024

f32 = jnp.float32
bf16 = jnp.bfloat16
DEVICES = ("energy", "slab")


def parts(matrix):
    high = matrix.astype(bf16)
    return high, (matrix - high.astype(f32)).astype(bf16)


def dot(left, right, transposed=False):
    contract = (((1,), (1 if transposed else 0,)), ((), ()))

    def multiply(a, b):
        return lax.dot_general(a, b, contract, preferred_element_type=f32)

    size = left[0].shape[0]
    both = multiply(jnp.concatenate(left, axis=0), right[0])
    return both[:size] + both[size:] + multiply(left[0], right[1])


def factor(matrix):
    return parts(matrix[0]), parts(matrix[1]), parts(matrix[0] + matrix[1])


def adjoint_factor(matrix):
    return parts(matrix[0]), parts(matrix[1]), parts(matrix[0] - matrix[1])


def product(left, right):
    real, imag, both = (dot(a, b) for a, b in zip(left, right))
    return real - imag, both - real - imag


def adjoint_product(left, right):
    real, imag, both = (dot(a, b, transposed=True) for a, b in zip(left, right))
    return real + imag, both - real + imag


def add(*matrices):
    return sum(m[0] for m in matrices), sum(m[1] for m in matrices)


def as_column(row):
    size = row.shape[1]
    return jnp.broadcast_to(row, (SUBLANES, size)).T[:, 0:1]


def start_of(energy, onsite, damping):
    real = energy - onsite
    modulus = real * real + damping * damping
    present = damping > 0.0
    modulus = jnp.where(present, modulus, 1.0)
    return jnp.where(present, real / modulus, 0.0), jnp.where(present, -damping / modulus, 0.0)


def scale(matrix, factor):
    return (
        matrix[0] * factor[0] - matrix[1] * factor[1],
        matrix[0] * factor[1] + matrix[1] * factor[0],
    )


def invert(coupled, row, column, between=()):
    given = None
    steps = iter(between)

    def beside():
        nonlocal given
        step = next(steps, None)
        if step is not None:
            given = step(given)

    b1 = scale(coupled, row)
    b1_factor = factor(b1)
    b2 = product(b1_factor, b1_factor)
    beside()
    b2_factor = factor(b2)
    b4 = product(b2_factor, b2_factor)
    b3 = product(b1_factor, b2_factor)
    beside()
    t = add(b1, b2, b3)
    rest = product(factor(t), factor(b4))
    size = b1[0].shape[0]
    unit = (
        lax.broadcasted_iota(jnp.int32, (size, size), 0)
        == lax.broadcasted_iota(jnp.int32, (size, size), 1)
    ).astype(f32)
    total = add(t, b4, rest)
    return scale((unit + total[0], total[1]), column), given


def halves(message_ref):
    height, columns = message_ref.shape
    return message_ref.at[pl.ds(columns, height - columns)], message_ref.at[pl.ds(0, columns)]


class Element:
    def __init__(self, message_refs, hopping_ref, onsite_ref, chain, total_energies):
        size = hopping_ref.shape[-1]
        parity = lax.rem(lax.axis_index("energy"), SHIFT)
        index = (SHIFT * chain + parity).astype(f32)
        energy = -2.0 + (4.0 / total_energies) * (index + 0.5)
        self.real_ref, self.imag_ref = (
            message_refs if len(message_refs) == 2 else halves(message_refs[0])
        )
        damping = self.real_ref[size : size + 1, :]
        self.occupation = self.real_ref[size + 1 : size + 2, :]
        onsite = onsite_ref[...]
        self.row = start_of(energy, onsite, damping)
        self.column = tuple(as_column(part) for part in self.row)
        self.hopping_ref = hopping_ref

    def sigma(self):
        size = self.hopping_ref.shape[-1]
        return self.real_ref[0:size, :], self.imag_ref[0:size, :]

    def coupled(self):
        real, imag = self.sigma()
        return self.hopping_ref[0] + real, imag

    def source(self):
        real, imag = self.sigma()
        return -self.occupation * (real - real.T), -self.occupation * (imag + imag.T)

    def green(self):
        return invert(self.coupled(), self.row, self.column)[0]

    def green_and_lesser(self, source):
        green = self.green()
        mixed = product(factor(green), factor(source))
        return green, adjoint_product(factor(mixed), adjoint_factor(green))

    def lesser_row(self, coupled, source, beyond):
        beyond_source = factor(beyond.source())
        beyond_green = beyond.green()
        steps = (
            lambda _: product(factor(beyond_green), beyond_source),
            lambda mixed: adjoint_product(factor(mixed), adjoint_factor(beyond_green)),
        )
        coupled = with_half(coupled, beyond_green)
        green, lesser = invert(coupled, self.row, self.column, steps)
        source = with_half(source, lesser)
        real, imag = parts(green[0]), parts(green[1])
        source_real, source_imag = parts(source[0]), parts(source[1])
        terms = green[0] * dot(real, source_imag) + green[1] * dot(imag, source_imag)
        terms = terms - 2.0 * green[1] * dot(real, source_real)
        column = jnp.sum(terms, axis=1, keepdims=True)
        return jnp.broadcast_to(column, (column.shape[0], LANES)).T[0:1, :]


def with_half(matrix, phonon):
    return tuple(a + PHONON * b for a, b in zip(matrix, phonon))


def load(ref):
    return ref[0], ref[1]


def store(ref, matrix):
    ref[0], ref[1] = matrix


def chain_places():
    here = lax.axis_index("energy")
    odd = lax.rem(here, 2)
    step = 1 - 2 * odd
    return {"own": here, "pair": here + step, "early": here + 2 * step, "late": here - step}


def vmem():
    return pl.BlockSpec(memory_space=pltpu.VMEM)


def call(kernel, operands, specs, shapes, **options):
    several = isinstance(shapes, list)
    return pl.pallas_call(
        kernel,
        out_shape=shapes,
        in_specs=specs,
        out_specs=[vmem() for _ in shapes] if several else vmem(),
        compiler_params=pltpu.CompilerParams(vmem_limit_bytes=VMEM_BYTES),
        cost_estimate=pl.CostEstimate(flops=0, transcendentals=0, bytes_accessed=0),
        **options,
    )(*operands)


def block_messages(boundary_green, coupling, damping, occupation):
    _, _, _, rows, columns = boundary_green.shape

    def kernel(block_ref, coupling_ref, *refs):
        level_refs, (real_ref, imag_ref), own_refs = refs[:2], refs[2:4], refs[4:6]
        own_levels_ref, held_refs, sems = refs[6], refs[7:9], refs[9]
        parity = lax.rem(lax.axis_index("energy"), SHIFT)
        moves = [
            *zip(level_refs, held_refs),
            (block_ref.at[0, 0, 1 - parity], real_ref.at[pl.ds(0, rows)]),
            (block_ref.at[1, 0, 1 - parity], imag_ref.at[pl.ds(0, rows)]),
            (block_ref.at[0, 0, parity], own_refs[0].at[pl.ds(0, rows)]),
            (coupling_ref, own_refs[0].at[pl.ds(rows, 1)]),
            (block_ref.at[1, 0, parity], own_refs[1].at[pl.ds(0, rows)]),
        ]
        copies = [
            pltpu.make_async_copy(source, target, sems.at[at])
            for at, (source, target) in enumerate(moves)
        ]
        for copy in copies:
            copy.start()
        for copy in copies[:2]:
            copy.wait()
        damping_here, occupation_here = (held_ref[...] for held_ref in held_refs)
        which = lax.broadcasted_iota(jnp.int32, (SUBLANES, columns), 0)
        levels = [
            jnp.where(which == 0, damping_here[:, at : at + 1], occupation_here[:, at : at + 1])
            for at in range(SHIFT)
        ]
        real_ref[rows : rows + SUBLANES, :] = jnp.where(parity == 0, levels[1], levels[0])
        own_levels_ref[...] = jnp.where(parity == 0, levels[0], levels[1])
        for copy in copies[2:]:
            copy.wait()

    operands = (boundary_green, coupling, damping, occupation)
    return call(
        kernel,
        [pltpu.with_memory_space_constraint(x, pltpu.HBM) for x in operands],
        [pl.BlockSpec(memory_space=pltpu.HBM)] * 4,
        [
            jax.ShapeDtypeStruct((height, columns), f32)
            for height in (*(rows + extra for extra in BELOW), SUBLANES)
        ],
        scratch_shapes=[
            pltpu.VMEM(damping.shape, f32),
            pltpu.VMEM(damping.shape, f32),
            pltpu.SemaphoreType.DMA((7,)),
        ],
    )


def slab_weights(coupling_ref, side_refs):
    even = lax.rem(lax.axis_index("slab"), 2) == 0
    below = coupling_ref.shape[1]
    weights = []
    for side_ref, before in zip(side_refs, (even, jnp.logical_not(even))):
        row = jnp.where(before, side_ref[below : below + 1, :], coupling_ref[...])
        weights.append(row * as_column(row))
    return weights


def own_self_energy(real_sides, imag_sides, coupling, levels):
    columns = coupling.shape[1]

    def kernel(*refs):
        real_refs, imag_refs = refs[:2], refs[2:4]
        coupling_ref, levels_ref, out_ref = refs[4:]
        weights = slab_weights(coupling_ref, real_refs)
        rows = pl.ds(0, columns)
        for low, side_refs in ((0, imag_refs), (columns, real_refs)):
            outer, inner = (w * ref[rows, :] for w, ref in zip(weights, side_refs))
            out_ref[pl.ds(low, columns), :] = outer + inner
        out_ref[2 * columns :, :] = levels_ref[...]

    return call(
        kernel,
        (*real_sides, *imag_sides, coupling, levels),
        [vmem()] * 6,
        jax.ShapeDtypeStruct((2 * columns + SUBLANES, columns), f32),
    )


def pair_self_energy(sides, coupling, own_sides, crossed, extra):
    columns = crossed.shape[1]
    height = columns + extra

    def kernel(outer_ref, inner_ref, coupling_ref, own_outer_ref, own_inner_ref, crossed_ref, out_ref):
        outer_weight, inner_weight = slab_weights(coupling_ref, (own_outer_ref, own_inner_ref))
        rows = pl.ds(0, columns)
        out_ref[rows, :] = outer_weight * outer_ref[rows, :] + inner_weight * inner_ref[rows, :]
        if extra:
            out_ref[columns:, :] = crossed_ref[columns:height, :]

    operands = (*sides, coupling, *own_sides, crossed)
    return call(kernel, operands, [vmem()] * 6, jax.ShapeDtypeStruct((height, columns), f32))


def own_first(message, hopping, onsite, total_energies):
    def kernel(message_ref, hopping_ref, onsite_ref, green_ref, lesser_ref, source_ref):
        place = chain_places()["own"]
        element = Element([message_ref], hopping_ref, onsite_ref, place, total_energies)
        source = element.source()
        green, lesser = element.green_and_lesser(source)
        for ref, matrix in ((green_ref, green), (lesser_ref, lesser), (source_ref, source)):
            store(ref, matrix)

    size = hopping.shape[-1]
    shape = jax.ShapeDtypeStruct((2, size, size), f32)
    return call(kernel, (message, hopping, onsite), [vmem()] * 3, [shape] * 3)


def pair_first(paired, mine, green, lesser, source, hopping, onsite, total_energies):
    def kernel(*refs):
        paired_refs, mine_refs, (green_ref, lesser_ref, source_ref) = refs[:2], refs[2:3], refs[3:6]
        hopping_ref, onsite_ref, *out_refs = refs[6:]
        chains = chain_places()
        pair = Element(paired_refs, hopping_ref, onsite_ref, chains["pair"], total_energies)
        own = Element(mine_refs, hopping_ref, onsite_ref, chains["own"], total_energies)
        pair_source = pair.source()
        store(out_refs[0], with_half(pair.coupled(), load(green_ref)))
        store(out_refs[1], with_half(pair_source, load(lesser_ref)))
        pair_green, pair_lesser = pair.green_and_lesser(pair_source)
        store(out_refs[2], with_half(own.coupled(), pair_green))
        store(out_refs[3], with_half(load(source_ref), pair_lesser))

    operands = (*paired, mine, green, lesser, source, hopping, onsite)
    size = hopping.shape[-1]
    shape = jax.ShapeDtypeStruct((2, size, size), f32)
    return call(kernel, operands, [vmem()] * len(operands), [shape] * 4)


def grid_share(rows_here, energy_devices):
    needed = rows_here + 2 * SWEEPS
    return needed, -(-2 * needed // energy_devices)


def pair_pass(early, paired, coupled, source, hopping, onsite, tile_map, potential, total_energies):
    size = hopping.shape[-1]
    energy_devices, slabs = lax.axis_size("energy"), lax.axis_size("slab")
    grid_total, columns = tile_map.shape[1:]
    rows_here = grid_total // energy_devices
    needed, share = grid_share(rows_here, energy_devices)
    rows = -(-needed // SUBLANES) * SUBLANES
    padded = grid_total + SUBLANES
    length = max(share * columns, size)

    def kernel(*refs):
        early_refs, paired_refs, refs = refs[:1], refs[1:3], refs[3:]
        coupled_ref, source_ref, hopping_ref, onsite_ref, tile_ref, potential_ref = refs[:6]
        parcel_ref, row_ref, local_ref, grid_ref = refs[6:]
        chains = chain_places()
        here = Element(paired_refs, hopping_ref, onsite_ref, chains["pair"], total_energies)
        beyond = Element(early_refs, hopping_ref, onsite_ref, chains["early"], total_energies)
        row = here.lesser_row(load(coupled_ref), load(source_ref), beyond)
        row_ref[...] = row
        at_energy, at_slab = lax.axis_index("energy"), lax.axis_index("slab")
        border = jnp.zeros((SUBLANES, columns), f32)
        for at, plane in enumerate((potential_ref[0], tile_ref[0].astype(f32))):
            low = at * padded
            grid_ref[low : low + SUBLANES, :] = border
            grid_ref[low + padded - SUBLANES : low + padded, :] = border
            grid_ref[low + SWEEPS : low + SWEEPS + grid_total, :] = plane
        for at in range(2):
            low = pl.multiple_of(at * padded + at_energy * rows_here, SUBLANES)
            local_ref[at] = grid_ref[pl.ds(low, rows), :]
        first = at_energy * share

        def filled(pieces):
            piece = jnp.concatenate(pieces, axis=1)
            short = length - piece.shape[1]
            if short:
                piece = jnp.concatenate([piece, jnp.zeros((1, short), f32)], axis=1)
            return piece

        same = filled([row])
        for to in range(energy_devices):
            pieces = []
            for i in range(share):
                place = jnp.minimum(first + i, 2 * needed - 1)
                which = (place >= needed).astype(jnp.int32)
                source = which * (padded - needed) + place + to * rows_here
                pieces.append(grid_ref[pl.ds(source, 1), :])
            other = filled(pieces)
            for slab in range(slabs):
                parcel_ref[to * slabs + slab, :, size:] = jnp.where(at_slab == slab, same, other)

    operands = [early, *paired, coupled, source, hopping, onsite, tile_map, potential]
    return call(
        kernel,
        operands,
        [vmem()] * len(operands),
        [
            jax.ShapeDtypeStruct((energy_devices * slabs, 1, size + length), f32),
            jax.ShapeDtypeStruct((1, size), f32),
            jax.ShapeDtypeStruct((2, rows, columns), f32),
        ],
        scratch_shapes=[pltpu.VMEM((2 * padded, columns), f32)],
    )


def own_pass(late, mine, coupled, source, hopping, onsite, parcels, other_row, total_energies):
    size = hopping.shape[-1]

    def kernel(*refs):
        late_refs, mine_refs, refs = refs[:2], refs[2:3], refs[3:]
        coupled_ref, source_ref, hopping_ref, onsite_ref, other_ref, _, parcel_ref, row_ref = refs
        chains = chain_places()
        here = Element(mine_refs, hopping_ref, onsite_ref, chains["own"], total_energies)
        beyond = Element(late_refs, hopping_ref, onsite_ref, chains["late"], total_energies)
        row = here.lesser_row(load(coupled_ref), load(source_ref), beyond)
        row_ref[...] = row
        both = row + other_ref[...]
        for to in range(parcel_ref.shape[0]):
            parcel_ref[to, :, 0:size] = both

    operands = [*late, mine, coupled, source, hopping, onsite, other_row, parcels]
    return call(
        kernel,
        operands,
        [vmem()] * len(operands),
        [
            jax.ShapeDtypeStruct(parcels.shape, f32),
            jax.ShapeDtypeStruct(other_row.shape, f32),
        ],
        input_output_aliases={len(operands) - 1: 0},
    )


def relax(parcels, own_row, local, orbitals, total_energies, grid_total, columns):
    energy_devices, slabs = parcels.shape[:2]
    rows_here = grid_total // energy_devices
    needed, share = grid_share(rows_here, energy_devices)
    rows = local.shape[1]

    def kernel(parcel_ref, own_ref, local_ref, lesser_ref, potential_ref, grid_ref):
        here, slab = lax.axis_index("energy"), lax.axis_index("slab")
        odd = lax.rem(here, 2)
        pair_row = parcel_ref[here + 1 - 2 * odd, slab, :, orbitals : 2 * orbitals]
        for parity in range(2):
            lesser_ref[0, parity : parity + 1, :] = jnp.where(
                odd == parity, own_ref[...], pair_row
            )
        empty = jnp.zeros((rows - needed, columns), f32)
        for at in range(slabs):
            for which in range(2):
                if rows > needed:
                    grid_ref[at, which, needed:, :] = empty
            for place in range(2 * needed):
                device, low = place // share, orbitals + place % share * columns
                row = place % needed
                grid_ref[at, place // needed, row : row + 1, :] = parcel_ref[
                    device, at, :, low : low + columns
                ]
        grid_ref[slab] = local_ref[...]
        grid_row = (
            lax.broadcasted_iota(jnp.int32, (rows, columns), 0) + here * rows_here - SWEEPS
        )
        inside = (grid_row >= 0) & (grid_row < grid_total)
        column = lax.broadcasted_iota(jnp.int32, (rows, columns), 1)
        sources, potentials = [], []
        for at in range(slabs):
            total = parcel_ref[0, at, :, 0:orbitals]
            for device in range(1, energy_devices):
                total = total + parcel_ref[device, at, :, 0:orbitals]
            density = (4.0 / total_energies) * total
            index = grid_ref[at, 1].astype(jnp.int32)
            found = jnp.zeros((rows, columns), f32)
            for low in range(0, orbitals, LANES):
                table = jnp.broadcast_to(density[:, low : low + LANES], (rows, LANES))
                within = jnp.clip(index - low, 0, LANES - 1)
                value = jnp.take_along_axis(table, within, axis=1)
                found = jnp.where((index >= low) & (index < low + LANES), value, found)
            sources.append(CHARGE * found)
            potentials.append(grid_ref[at, 0])
        pivots = [MAIN_DIAGONAL]
        for at in range(1, slabs):
            pivots.append(MAIN_DIAGONAL - 1.0 / pivots[-1])
        for sweep in range(SWEEPS):
            eliminated = []
            for at in range(slabs):
                p = potentials[at]
                beside = (
                    pltpu.roll(p, 1, 0)
                    + pltpu.roll(p, rows - 1, 0)
                    + jnp.where(column == 0, 0.0, pltpu.roll(p, 1, 1))
                    + jnp.where(column == columns - 1, 0.0, pltpu.roll(p, columns - 1, 1))
                )
                right = sources[at] + ANISO * beside
                if at:
                    right = right + (1.0 / pivots[at - 1]) * eliminated[-1]
                eliminated.append(right)
            after = None
            for at in reversed(range(slabs)):
                value = eliminated[at] if after is None else eliminated[at] + after
                after = value * (1.0 / pivots[at])
                potentials[at] = jnp.where(inside, after, 0.0)
        for at in range(slabs):
            grid_ref[at, 0] = potentials[at]
        potential_ref[0] = grid_ref[slab, 0, SWEEPS : SWEEPS + rows_here, :]

    return call(
        kernel,
        (parcels, own_row, local),
        [vmem()] * 3,
        [
            jax.ShapeDtypeStruct((1, 2, orbitals), f32),
            jax.ShapeDtypeStruct((1, rows_here, columns), f32),
        ],
        scratch_shapes=[pltpu.VMEM((slabs, 2, rows, columns), f32)],
    )


def per_device(
    onsite, hopping, coupling, boundary_green, damping, occupation, tile_map, prev_potential
):
    energy_devices, slabs = lax.axis_size("energy"), lax.axis_size("slab")
    orbitals = onsite.shape[1]
    assert boundary_green.shape[2] == SHIFT and energy_devices % 2 == 0
    total_energies = SHIFT * energy_devices

    swaps = [
        [pair for i in range(low, slabs - 1, 2) for pair in ((i, i + 1), (i + 1, i))]
        for low in (1, 0)
    ]
    last = energy_devices - 1
    pair = [(i, i ^ 1) for i in range(energy_devices)]
    far = [(i, i + 2) for i in range(1, last, 2) if i + 2 <= last]
    far += [(i, i - 2) for i in range(2, energy_devices, 2)]
    near = [(to, i) for i, to in far]

    common = (hopping, onsite)
    blocks = block_messages(boundary_green, coupling, damping, occupation)
    crossed = [lax.ppermute(part, "energy", pair) for part in blocks[:2]]
    own_sides = [[lax.ppermute(part, "slab", way) for way in swaps] for part in blocks[2:4]]
    mine = own_self_energy(*own_sides, coupling, blocks[4])
    early = lax.ppermute(mine, "energy", far)
    own_green, own_lesser, own_source = own_first(mine, *common, total_energies)
    paired, late = [], []
    for plane, part in enumerate(crossed):
        sides = [lax.ppermute(part, "slab", way) for way in swaps]
        if plane:
            part, own_green = lax.optimization_barrier((part, own_green))
        extra = 0 if plane else SUBLANES
        paired.append(pair_self_energy(sides, coupling, own_sides[0], part, extra))
        late.append(lax.ppermute(paired[-1], "energy", near))
    *pair_parts, own_coupled, own_total = pair_first(
        paired, mine, own_green, own_lesser, own_source, *common, total_energies
    )
    parcels, pair_row, local = pair_pass(
        early, paired, *pair_parts, *common, tile_map, prev_potential, total_energies
    )
    parcels, own_row = own_pass(
        late, mine, own_coupled, own_total, *common, parcels, pair_row, total_energies
    )
    parcels = lax.all_to_all(parcels, DEVICES, 0, 0)
    parcels = parcels.reshape(energy_devices, slabs, *parcels.shape[1:])
    return relax(parcels, own_row, local, orbitals, total_energies, *tile_map.shape[1:])


def solution(mesh):
    in_specs = (
        P("slab", None),
        P("slab", None, None),
        P("slab", None),
        P(None, "slab", "energy", None, None),
        P("slab", "energy"),
        P("slab", "energy"),
        P("slab", None, None),
        P("slab", None, None),
    )
    out_specs = (P("slab", "energy", None), P("slab", "energy", None))
    return jax.shard_map(
        per_device, mesh=mesh, in_specs=in_specs, out_specs=out_specs, check_vma=False
    )
```

```python
import functools

import jax
import jax.numpy as jnp
from jax import lax
from jax.experimental import pallas as pl
from jax.experimental.pallas import tpu as pltpu
from jax.sharding import PartitionSpec as P

SHIFT = 2
SWEEPS = 2
PHONON = 0.5
CHARGE = 2.0
ANISO = 0.05
SCREEN = 0.05
MAIN_DIAGONAL = 2.0 + 4.0 * ANISO + SCREEN
LANES = 128
SUBLANES = 8
BELOW = (8, 0, 24, 16)
VMEM_BYTES = 48 * 1024 * 1024

f32 = jnp.float32
bf16 = jnp.bfloat16
DEVICES = ("energy", "slab")


def parts(matrix):
    high = matrix.astype(bf16)
    return high, (matrix - high.astype(f32)).astype(bf16)


def dot(left, right, transposed=False):
    contract = (((1,), (1 if transposed else 0,)), ((), ()))

    def multiply(a, b):
        return lax.dot_general(a, b, contract, preferred_element_type=f32)

    size = left[0].shape[0]
    both = multiply(jnp.concatenate(left, axis=0), right[0])
    return both[:size] + both[size:] + multiply(left[0], right[1])


def factor(matrix):
    return parts(matrix[0]), parts(matrix[1]), parts(matrix[0] + matrix[1])


def adjoint_factor(matrix):
    return parts(matrix[0]), parts(matrix[1]), parts(matrix[0] - matrix[1])


def product(left, right):
    real, imag, both = (dot(a, b) for a, b in zip(left, right))
    return real - imag, both - real - imag


def adjoint_product(left, right):
    real, imag, both = (dot(a, b, transposed=True) for a, b in zip(left, right))
    return real + imag, both - real + imag


def add(*matrices):
    return sum(m[0] for m in matrices), sum(m[1] for m in matrices)


def as_column(row):
    size = row.shape[1]
    return jnp.broadcast_to(row, (SUBLANES, size)).T[:, 0:1]


def start_of(energy, onsite, damping):
    real = energy - onsite
    modulus = real * real + damping * damping
    present = damping > 0.0
    modulus = jnp.where(present, modulus, 1.0)
    return jnp.where(present, real / modulus, 0.0), jnp.where(present, -damping / modulus, 0.0)


def scale(matrix, factor):
    return (
        matrix[0] * factor[0] - matrix[1] * factor[1],
        matrix[0] * factor[1] + matrix[1] * factor[0],
    )


def invert(coupled, row, column, between=()):
    given = None
    steps = iter(between)

    def beside():
        nonlocal given
        step = next(steps, None)
        if step is not None:
            given = step(given)

    b1 = scale(coupled, row)
    b1_factor = factor(b1)
    b2 = product(b1_factor, b1_factor)
    beside()
    b2_factor = factor(b2)
    b4 = product(b2_factor, b2_factor)
    b3 = product(b1_factor, b2_factor)
    beside()
    t = add(b1, b2, b3)
    rest = product(factor(t), factor(b4))
    size = b1[0].shape[0]
    unit = (
        lax.broadcasted_iota(jnp.int32, (size, size), 0)
        == lax.broadcasted_iota(jnp.int32, (size, size), 1)
    ).astype(f32)
    total = add(t, b4, rest)
    return scale((unit + total[0], total[1]), column), given


def halves(message_ref):
    height, columns = message_ref.shape
    return message_ref.at[pl.ds(columns, height - columns)], message_ref.at[pl.ds(0, columns)]


class Element:
    def __init__(self, message_refs, hopping_ref, onsite_ref, chain, total_energies):
        size = hopping_ref.shape[-1]
        parity = lax.rem(lax.axis_index("energy"), SHIFT)
        index = (SHIFT * chain + parity).astype(f32)
        energy = -2.0 + (4.0 / total_energies) * (index + 0.5)
        self.real_ref, self.imag_ref = (
            message_refs if len(message_refs) == 2 else halves(message_refs[0])
        )
        damping = self.real_ref[size : size + 1, :]
        self.occupation = self.real_ref[size + 1 : size + 2, :]
        onsite = onsite_ref[...]
        self.row = start_of(energy, onsite, damping)
        self.column = tuple(as_column(part) for part in self.row)
        self.hopping_ref = hopping_ref

    def sigma(self):
        size = self.hopping_ref.shape[-1]
        return self.real_ref[0:size, :], self.imag_ref[0:size, :]

    def coupled(self):
        real, imag = self.sigma()
        return self.hopping_ref[0] + real, imag

    def source(self):
        real, imag = self.sigma()
        return -self.occupation * (real - real.T), -self.occupation * (imag + imag.T)

    def green(self):
        return invert(self.coupled(), self.row, self.column)[0]

    def green_and_lesser(self, source):
        green = self.green()
        mixed = product(factor(green), factor(source))
        return green, adjoint_product(factor(mixed), adjoint_factor(green))

    def lesser_row(self, coupled, source, beyond):
        beyond_source = factor(beyond.source())
        beyond_green = beyond.green()
        steps = (
            lambda _: product(factor(beyond_green), beyond_source),
            lambda mixed: adjoint_product(factor(mixed), adjoint_factor(beyond_green)),
        )
        coupled = with_half(coupled, beyond_green)
        green, lesser = invert(coupled, self.row, self.column, steps)
        source = with_half(source, lesser)
        real, imag = parts(green[0]), parts(green[1])
        source_real, source_imag = parts(source[0]), parts(source[1])
        terms = green[0] * dot(real, source_imag) + green[1] * dot(imag, source_imag)
        terms = terms - 2.0 * green[1] * dot(real, source_real)
        column = jnp.sum(terms, axis=1, keepdims=True)
        return jnp.broadcast_to(column, (column.shape[0], LANES)).T[0:1, :]


def with_half(matrix, phonon):
    return tuple(a + PHONON * b for a, b in zip(matrix, phonon))


def load(ref):
    return ref[0], ref[1]


def store(ref, matrix):
    ref[0], ref[1] = matrix


def chain_places():
    here = lax.axis_index("energy")
    odd = lax.rem(here, 2)
    step = 1 - 2 * odd
    return {"own": here, "pair": here + step, "early": here + 2 * step, "late": here - step}


def vmem():
    return pl.BlockSpec(memory_space=pltpu.VMEM)


def call(kernel, operands, specs, shapes, **options):
    several = isinstance(shapes, list)
    return pl.pallas_call(
        kernel,
        out_shape=shapes,
        in_specs=specs,
        out_specs=[vmem() for _ in shapes] if several else vmem(),
        compiler_params=pltpu.CompilerParams(vmem_limit_bytes=VMEM_BYTES),
        cost_estimate=pl.CostEstimate(flops=0, transcendentals=0, bytes_accessed=0),
        **options,
    )(*operands)


def block_messages(boundary_green, coupling, damping, occupation):
    _, _, _, rows, columns = boundary_green.shape

    def kernel(block_ref, coupling_ref, *refs):
        level_refs, (real_ref, imag_ref), own_refs = refs[:2], refs[2:4], refs[4:6]
        own_levels_ref, held_refs, sems = refs[6], refs[7:9], refs[9]
        parity = lax.rem(lax.axis_index("energy"), SHIFT)
        moves = [
            *zip(level_refs, held_refs),
            (block_ref.at[0, 0, 1 - parity], real_ref.at[pl.ds(0, rows)]),
            (block_ref.at[1, 0, 1 - parity], imag_ref.at[pl.ds(0, rows)]),
            (block_ref.at[0, 0, parity], own_refs[0].at[pl.ds(0, rows)]),
            (coupling_ref, own_refs[0].at[pl.ds(rows, 1)]),
            (block_ref.at[1, 0, parity], own_refs[1].at[pl.ds(0, rows)]),
        ]
        copies = [
            pltpu.make_async_copy(source, target, sems.at[at])
            for at, (source, target) in enumerate(moves)
        ]
        for copy in copies:
            copy.start()
        for copy in copies[:2]:
            copy.wait()
        damping_here, occupation_here = (held_ref[...] for held_ref in held_refs)
        which = lax.broadcasted_iota(jnp.int32, (SUBLANES, columns), 0)
        levels = [
            jnp.where(which == 0, damping_here[:, at : at + 1], occupation_here[:, at : at + 1])
            for at in range(SHIFT)
        ]
        real_ref[rows : rows + SUBLANES, :] = jnp.where(parity == 0, levels[1], levels[0])
        own_levels_ref[...] = jnp.where(parity == 0, levels[0], levels[1])
        for copy in copies[2:]:
            copy.wait()

    operands = (boundary_green, coupling, damping, occupation)
    return call(
        kernel,
        [pltpu.with_memory_space_constraint(x, pltpu.HBM) for x in operands],
        [pl.BlockSpec(memory_space=pltpu.HBM)] * 4,
        [
            jax.ShapeDtypeStruct((height, columns), f32)
            for height in (*(rows + extra for extra in BELOW), SUBLANES)
        ],
        scratch_shapes=[
            pltpu.VMEM(damping.shape, f32),
            pltpu.VMEM(damping.shape, f32),
            pltpu.SemaphoreType.DMA((7,)),
        ],
    )


def slab_weights(coupling_ref, side_refs):
    even = lax.rem(lax.axis_index("slab"), 2) == 0
    below = coupling_ref.shape[1]
    weights = []
    for side_ref, before in zip(side_refs, (even, jnp.logical_not(even))):
        row = jnp.where(before, side_ref[below : below + 1, :], coupling_ref[...])
        weights.append(row * as_column(row))
    return weights


def own_self_energy(real_sides, imag_sides, coupling, levels):
    columns = coupling.shape[1]

    def kernel(*refs):
        real_refs, imag_refs = refs[:2], refs[2:4]
        coupling_ref, levels_ref, out_ref = refs[4:]
        weights = slab_weights(coupling_ref, real_refs)
        rows = pl.ds(0, columns)
        for low, side_refs in ((0, imag_refs), (columns, real_refs)):
            outer, inner = (w * ref[rows, :] for w, ref in zip(weights, side_refs))
            out_ref[pl.ds(low, columns), :] = outer + inner
        out_ref[2 * columns :, :] = levels_ref[...]

    return call(
        kernel,
        (*real_sides, *imag_sides, coupling, levels),
        [vmem()] * 6,
        jax.ShapeDtypeStruct((2 * columns + SUBLANES, columns), f32),
    )


def pair_self_energy(sides, coupling, own_sides, crossed, extra):
    columns = crossed.shape[1]
    height = columns + extra

    def kernel(outer_ref, inner_ref, coupling_ref, own_outer_ref, own_inner_ref, crossed_ref, out_ref):
        outer_weight, inner_weight = slab_weights(coupling_ref, (own_outer_ref, own_inner_ref))
        rows = pl.ds(0, columns)
        out_ref[rows, :] = outer_weight * outer_ref[rows, :] + inner_weight * inner_ref[rows, :]
        if extra:
            out_ref[columns:, :] = crossed_ref[columns:height, :]

    operands = (*sides, coupling, *own_sides, crossed)
    return call(kernel, operands, [vmem()] * 6, jax.ShapeDtypeStruct((height, columns), f32))


def own_first(message, hopping, onsite, total_energies):
    def kernel(message_ref, hopping_ref, onsite_ref, green_ref, lesser_ref, source_ref):
        place = chain_places()["own"]
        element = Element([message_ref], hopping_ref, onsite_ref, place, total_energies)
        source = element.source()
        green, lesser = element.green_and_lesser(source)
        for ref, matrix in ((green_ref, green), (lesser_ref, lesser), (source_ref, source)):
            store(ref, matrix)

    size = hopping.shape[-1]
    shape = jax.ShapeDtypeStruct((2, size, size), f32)
    return call(kernel, (message, hopping, onsite), [vmem()] * 3, [shape] * 3)


def pair_first(paired, mine, green, lesser, source, hopping, onsite, total_energies):
    def kernel(*refs):
        paired_refs, mine_refs, (green_ref, lesser_ref, source_ref) = refs[:2], refs[2:3], refs[3:6]
        hopping_ref, onsite_ref, *out_refs = refs[6:]
        chains = chain_places()
        pair = Element(paired_refs, hopping_ref, onsite_ref, chains["pair"], total_energies)
        own = Element(mine_refs, hopping_ref, onsite_ref, chains["own"], total_energies)
        pair_source = pair.source()
        store(out_refs[0], with_half(pair.coupled(), load(green_ref)))
        store(out_refs[1], with_half(pair_source, load(lesser_ref)))
        pair_green, pair_lesser = pair.green_and_lesser(pair_source)
        store(out_refs[2], with_half(own.coupled(), pair_green))
        store(out_refs[3], with_half(load(source_ref), pair_lesser))

    operands = (*paired, mine, green, lesser, source, hopping, onsite)
    size = hopping.shape[-1]
    shape = jax.ShapeDtypeStruct((2, size, size), f32)
    return call(kernel, operands, [vmem()] * len(operands), [shape] * 4)


def grid_share(rows_here, energy_devices):
    needed = rows_here + 2 * SWEEPS
    return needed, -(-2 * needed // energy_devices)


def pair_pass(early, paired, coupled, source, hopping, onsite, tile_map, potential, total_energies):
    size = hopping.shape[-1]
    energy_devices, slabs = lax.axis_size("energy"), lax.axis_size("slab")
    grid_total, columns = tile_map.shape[1:]
    rows_here = grid_total // energy_devices
    needed, share = grid_share(rows_here, energy_devices)
    rows = -(-needed // SUBLANES) * SUBLANES
    padded = grid_total + SUBLANES
    length = max(share * columns, size)

    def kernel(*refs):
        early_refs, paired_refs, refs = refs[:1], refs[1:3], refs[3:]
        coupled_ref, source_ref, hopping_ref, onsite_ref, tile_ref, potential_ref = refs[:6]
        parcel_ref, row_ref, local_ref, grid_ref = refs[6:]
        chains = chain_places()
        here = Element(paired_refs, hopping_ref, onsite_ref, chains["pair"], total_energies)
        beyond = Element(early_refs, hopping_ref, onsite_ref, chains["early"], total_energies)
        row = here.lesser_row(load(coupled_ref), load(source_ref), beyond)
        row_ref[...] = row
        at_energy, at_slab = lax.axis_index("energy"), lax.axis_index("slab")
        border = jnp.zeros((SUBLANES, columns), f32)
        for at, plane in enumerate((potential_ref[0], tile_ref[0].astype(f32))):
            low = at * padded
            grid_ref[low : low + SUBLANES, :] = border
            grid_ref[low + padded - SUBLANES : low + padded, :] = border
            grid_ref[low + SWEEPS : low + SWEEPS + grid_total, :] = plane
        for at in range(2):
            low = pl.multiple_of(at * padded + at_energy * rows_here, SUBLANES)
            local_ref[at] = grid_ref[pl.ds(low, rows), :]
        first = at_energy * share

        def filled(pieces):
            piece = jnp.concatenate(pieces, axis=1)
            short = length - piece.shape[1]
            if short:
                piece = jnp.concatenate([piece, jnp.zeros((1, short), f32)], axis=1)
            return piece

        same = filled([row])
        for to in range(energy_devices):
            pieces = []
            for i in range(share):
                place = jnp.minimum(first + i, 2 * needed - 1)
                which = (place >= needed).astype(jnp.int32)
                source = which * (padded - needed) + place + to * rows_here
                pieces.append(grid_ref[pl.ds(source, 1), :])
            other = filled(pieces)
            for slab in range(slabs):
                parcel_ref[to * slabs + slab, :, size:] = jnp.where(at_slab == slab, same, other)

    operands = [early, *paired, coupled, source, hopping, onsite, tile_map, potential]
    return call(
        kernel,
        operands,
        [vmem()] * len(operands),
        [
            jax.ShapeDtypeStruct((energy_devices * slabs, 1, size + length), f32),
            jax.ShapeDtypeStruct((1, size), f32),
            jax.ShapeDtypeStruct((2, rows, columns), f32),
        ],
        scratch_shapes=[pltpu.VMEM((2 * padded, columns), f32)],
    )


def own_pass(late, mine, coupled, source, hopping, onsite, parcels, other_row, total_energies):
    size = hopping.shape[-1]

    def kernel(*refs):
        late_refs, mine_refs, refs = refs[:2], refs[2:3], refs[3:]
        coupled_ref, source_ref, hopping_ref, onsite_ref, other_ref, _, parcel_ref, row_ref = refs
        chains = chain_places()
        here = Element(mine_refs, hopping_ref, onsite_ref, chains["own"], total_energies)
        beyond = Element(late_refs, hopping_ref, onsite_ref, chains["late"], total_energies)
        row = here.lesser_row(load(coupled_ref), load(source_ref), beyond)
        row_ref[...] = row
        both = row + other_ref[...]
        for to in range(parcel_ref.shape[0]):
            parcel_ref[to, :, 0:size] = both

    operands = [*late, mine, coupled, source, hopping, onsite, other_row, parcels]
    return call(
        kernel,
        operands,
        [vmem()] * len(operands),
        [
            jax.ShapeDtypeStruct(parcels.shape, f32),
            jax.ShapeDtypeStruct(other_row.shape, f32),
        ],
        input_output_aliases={len(operands) - 1: 0},
    )


def relax(parcels, own_row, local, orbitals, total_energies, grid_total, columns):
    energy_devices, slabs = parcels.shape[:2]
    rows_here = grid_total // energy_devices
    needed, share = grid_share(rows_here, energy_devices)
    rows = local.shape[1]

    def kernel(parcel_ref, own_ref, local_ref, lesser_ref, potential_ref, grid_ref):
        here, slab = lax.axis_index("energy"), lax.axis_index("slab")
        odd = lax.rem(here, 2)
        pair_row = parcel_ref[here + 1 - 2 * odd, slab, :, orbitals : 2 * orbitals]
        for parity in range(2):
            lesser_ref[0, parity : parity + 1, :] = jnp.where(
                odd == parity, own_ref[...], pair_row
            )
        empty = jnp.zeros((rows - needed, columns), f32)
        for at in range(slabs):
            for which in range(2):
                if rows > needed:
                    grid_ref[at, which, needed:, :] = empty
            for place in range(2 * needed):
                device, low = place // share, orbitals + place % share * columns
                row = place % needed
                grid_ref[at, place // needed, row : row + 1, :] = parcel_ref[
                    device, at, :, low : low + columns
                ]
        grid_ref[slab] = local_ref[...]
        grid_row = (
            lax.broadcasted_iota(jnp.int32, (rows, columns), 0) + here * rows_here - SWEEPS
        )
        inside = (grid_row >= 0) & (grid_row < grid_total)
        column = lax.broadcasted_iota(jnp.int32, (rows, columns), 1)
        sources, potentials = [], []
        for at in range(slabs):
            total = parcel_ref[0, at, :, 0:orbitals]
            for device in range(1, energy_devices):
                total = total + parcel_ref[device, at, :, 0:orbitals]
            density = (4.0 / total_energies) * total
            index = grid_ref[at, 1].astype(jnp.int32)
            found = jnp.zeros((rows, columns), f32)
            for low in range(0, orbitals, LANES):
                table = jnp.broadcast_to(density[:, low : low + LANES], (rows, LANES))
                within = jnp.clip(index - low, 0, LANES - 1)
                value = jnp.take_along_axis(table, within, axis=1)
                found = jnp.where((index >= low) & (index < low + LANES), value, found)
            sources.append(CHARGE * found)
            potentials.append(grid_ref[at, 0])
        pivots = [MAIN_DIAGONAL]
        for at in range(1, slabs):
            pivots.append(MAIN_DIAGONAL - 1.0 / pivots[-1])
        for sweep in range(SWEEPS):
            eliminated = []
            for at in range(slabs):
                p = potentials[at]
                beside = (
                    pltpu.roll(p, 1, 0)
                    + pltpu.roll(p, rows - 1, 0)
                    + jnp.where(column == 0, 0.0, pltpu.roll(p, 1, 1))
                    + jnp.where(column == columns - 1, 0.0, pltpu.roll(p, columns - 1, 1))
                )
                right = sources[at] + ANISO * beside
                if at:
                    right = right + (1.0 / pivots[at - 1]) * eliminated[-1]
                eliminated.append(right)
            after = None
            for at in reversed(range(slabs)):
                value = eliminated[at] if after is None else eliminated[at] + after
                after = value * (1.0 / pivots[at])
                potentials[at] = jnp.where(inside, after, 0.0)
        for at in range(slabs):
            grid_ref[at, 0] = potentials[at]
        potential_ref[0] = grid_ref[slab, 0, SWEEPS : SWEEPS + rows_here, :]

    return call(
        kernel,
        (parcels, own_row, local),
        [vmem()] * 3,
        [
            jax.ShapeDtypeStruct((1, 2, orbitals), f32),
            jax.ShapeDtypeStruct((1, rows_here, columns), f32),
        ],
        scratch_shapes=[pltpu.VMEM((slabs, 2, rows, columns), f32)],
    )


def per_device(
    onsite, hopping, coupling, boundary_green, damping, occupation, tile_map, prev_potential
):
    energy_devices, slabs = lax.axis_size("energy"), lax.axis_size("slab")
    orbitals = onsite.shape[1]
    assert boundary_green.shape[2] == SHIFT and energy_devices % 2 == 0
    total_energies = SHIFT * energy_devices

    swaps = [
        [pair for i in range(low, slabs - 1, 2) for pair in ((i, i + 1), (i + 1, i))]
        for low in (1, 0)
    ]
    last = energy_devices - 1
    pair = [(i, i ^ 1) for i in range(energy_devices)]
    far = [(i, i + 2) for i in range(1, last, 2) if i + 2 <= last]
    far += [(i, i - 2) for i in range(2, energy_devices, 2)]
    near = [(to, i) for i, to in far]

    common = (hopping, onsite)
    blocks = block_messages(boundary_green, coupling, damping, occupation)
    crossed = [lax.ppermute(part, "energy", pair) for part in blocks[:2]]
    own_sides = [[lax.ppermute(part, "slab", way) for way in swaps] for part in blocks[2:4]]
    mine = own_self_energy(*own_sides, coupling, blocks[4])
    early = lax.ppermute(mine, "energy", far)
    own_green, own_lesser, own_source = own_first(mine, *common, total_energies)
    paired, late = [], []
    for plane, part in enumerate(crossed):
        sides = [lax.ppermute(part, "slab", way) for way in swaps]
        if plane:
            part, own_green = lax.optimization_barrier((part, own_green))
        extra = 0 if plane else SUBLANES
        paired.append(pair_self_energy(sides, coupling, own_sides[0], part, extra))
        late.append(lax.ppermute(paired[-1], "energy", near))
    *pair_parts, own_coupled, own_total = pair_first(
        paired, mine, own_green, own_lesser, own_source, *common, total_energies
    )
    parcels, pair_row, local = pair_pass(
        early, paired, *pair_parts, *common, tile_map, prev_potential, total_energies
    )
    parcels, own_row = own_pass(
        late, mine, own_coupled, own_total, *common, parcels, pair_row, total_energies
    )
    parcels = lax.all_to_all(parcels, DEVICES, 0, 0)
    parcels = parcels.reshape(energy_devices, slabs, *parcels.shape[1:])
    return relax(parcels, own_row, local, orbitals, total_energies, *tile_map.shape[1:])


def solution(mesh):
    in_specs = (
        P("slab", None),
        P("slab", None, None),
        P("slab", None),
        P(None, "slab", "energy", None, None),
        P("slab", "energy"),
        P("slab", "energy"),
        P("slab", None, None),
        P("slab", None, None),
    )
    out_specs = (P("slab", "energy", None), P("slab", "energy", None))
    return jax.shard_map(
        per_device, mesh=mesh, in_specs=in_specs, out_specs=out_specs, check_vma=False
    )
```
